128 devices in a mesh: states: 64 (over z, y, x), act: 2 (over core).
Axes of the slice: x: 4, y: 4, z: 4, core: 2. Of those that a mesh axis runs over, the one named last changes fastest.
Arguments:
- transitions: float32 [4, 1024, 2, 128, 128], P('act', 'states'), may hold values from 7.8125e-05 to 0.01953125
- columns: int32 [4, 1024, 2], P(None, 'states'), may hold values from 0 to 1023, as said below
- targets: int32 [131072, 128], P('states'), may hold values 0 or 1
Outputs:
- values: float32 [131072, 128], P('states')
The draws below stay inside these ranges and needn't reach their ends.
Inputs may be any that keep to these rules, and one draw needn't show every extreme that they name: columns[a, b, t] = (b + d) mod 1024 with |d| <= 8; both d = 8 and d = -8 occur in every draw.
All inputs are finite; a program needn't handle non-finite values. No bound on the sum of `targets` on one device may be relied on, other than what follows from the above.
Results may differ from the reference program's by a relative error of at most 0.0003.
Values sent between devices are 32-bit elements; how exact they have to be, the bound alone decides.
A program may use at most 64 MiB of HBM per device.

```python
import math
import jax
import jax.numpy as jnp
from jax import lax

TILE = 128
K = 128
ACTIONS = 4
REACH = 8
SWEEPS = 12
RB_DEV = 16
BLOCKS = 1024
NSTATES = 131072


def draw_columns(key, part):
    offsets = jax.random.randint(key, (ACTIONS, BLOCKS, 2), -REACH, REACH + 1)
    upper_rows = jax.random.randint(jax.random.fold_in(key, 11), (ACTIONS,), 0, BLOCKS)
    lower_rows = jax.random.randint(jax.random.fold_in(key, 12), (ACTIONS,), 0, BLOCKS)
    action_ids = jnp.arange(ACTIONS, dtype=jnp.int32)
    offsets = offsets.at[action_ids, upper_rows, 0].set(REACH)
    offsets = offsets.at[action_ids, lower_rows, 1].set(-REACH)
    row_ids = jnp.arange(BLOCKS, dtype=jnp.int32)[None, :, None]
    return ((row_ids + offsets) % BLOCKS).astype(jnp.int32)


def set_ends(result, stream_key, least, high):
    longest = result.shape.index(max(result.shape))
    spots = []
    for shift in (0, 1):
        where = [jax.random.randint(jax.random.fold_in(stream_key, axis), (), 0, length) for axis, length in enumerate(result.shape)]
        where[longest] = (where[longest] + shift) % result.shape[longest]
        spots.append(tuple(where))
    return result.at[spots[0]].set(least).at[spots[1]].set(high)


def steps_of(rng, dims, split, low, high):
    level = 1.0
    for dim, shards_of in split:
        heights = jax.random.uniform(jax.random.fold_in(jax.random.fold_in(rng, 6), dim), (shards_of,), jnp.float32, low / len(split), high / len(split))
        level = level * jnp.repeat(jnp.exp(heights), dims[dim] // shards_of).reshape((-1,) + (1,) * (len(dims) - 1 - dim))
    return level


def setup_inputs(seed: int = 0) -> dict:
    seeds = jax.random.split(jax.random.key(seed), 4)
    transitions = jnp.clip(jnp.exp(math.log(0.01953125) - 5.521461 * jax.random.uniform(seeds[0], (ACTIONS, BLOCKS, 2, TILE, TILE), jnp.float32) ** steps_of(seeds[0], (ACTIONS, BLOCKS, 2, TILE, TILE), ((0, 2), (1, 64)), -0.2, 0.2)), 7.812499825377017e-05, 0.01953125)
    columns = draw_columns(jax.random.fold_in(seeds[3], 71), 0)
    targets = set_ends((jax.random.randint(seeds[2], (NSTATES, K), 0, 8) < 1).astype(jnp.int32), jax.random.fold_in(seeds[2], 1), 0, 1)
    return {"transitions": transitions, "columns": columns, "targets": targets}


def reference(transitions, columns, targets):
    hits = targets == 1
    panel = targets.astype(jnp.float32)
    group_count = BLOCKS // RB_DEV
    for sweep_index in range(SWEEPS):
        blocks = panel.reshape(BLOCKS, TILE, K)

        def one_group(group_index):
            first_row = (group_index * RB_DEV).astype(jnp.int32)
            tiles = lax.dynamic_slice_in_dim(transitions, first_row, RB_DEV, 1)
            column_ids = lax.dynamic_slice_in_dim(columns, first_row, RB_DEV, 1)
            picked = blocks[column_ids]
            products = jnp.einsum("arbij,arbjk->arik", tiles, picked, precision=lax.Precision.HIGHEST)
            return jnp.max(products, axis=0)

        largest = lax.map(one_group, jnp.arange(group_count, dtype=jnp.int32))
        panel = jnp.where(hits, jnp.float32(1.0), largest.reshape(NSTATES, K))
    return panel
```

```python
import functools

import jax
import jax.numpy as jnp
from jax import lax
from jax.experimental import pallas as pl
from jax.experimental.pallas import tpu as pltpu
from jax.sharding import PartitionSpec as P

REACH = 8
SWEEPS = 12
MESH = pl.DeviceIdType.MESH


def sweep_kernel(n_states, pos_ref, trans_hbm, tgt_ref, out_ref,
                 win0, win1, t_own, t_oth, tsem, send_sem, recv_sem):
    i = lax.axis_index("states")
    c = lax.axis_index("act")
    half = t_own.shape[1]
    tile = t_own.shape[3]
    own_pos = half + half * c
    part_pos = 2 * half - half * c
    halo_pos = 3 * half * c
    nb_halo_pos = 3 * half * (1 - c)
    partner = (i, 1 - c)
    neighbour = (lax.rem(i + 2 * c - 1 + n_states, n_states), 1 - c)

    barrier = pltpu.get_barrier_semaphore()
    for dev in (partner, neighbour):
        pl.semaphore_signal(barrier, inc=1, device_id=dev, device_id_type=MESH)
    pl.semaphore_wait(barrier, 2)

    own_copy = pltpu.make_async_copy(trans_hbm.at[:, pl.ds(half * c, half)], t_own, tsem.at[0])
    own_copy.start()
    oth_copy = pltpu.make_async_remote_copy(
        src_ref=trans_hbm.at[:, pl.ds(half * (1 - c), half)], dst_ref=t_oth,
        send_sem=tsem.at[1], recv_sem=tsem.at[2], device_id=partner, device_id_type=MESH)
    oth_copy.start()

    win0[pl.ds(half, 2 * half)] = tgt_ref[...].astype(jnp.float32)
    init = pltpu.make_async_remote_copy(
        src_ref=win0.at[pl.ds(own_pos, half)], dst_ref=win0.at[pl.ds(nb_halo_pos, half)],
        send_sem=send_sem.at[0, 1], recv_sem=recv_sem.at[0, 1],
        device_id=neighbour, device_id_type=MESH)
    init.start()
    init.wait_send()
    init.wait_recv()
    own_copy.wait()
    oth_copy.wait_send()
    oth_copy.wait_recv()

    def sweep(src, dst, slot):
        def block(jj, carry):
            j = half * c + jj
            best = None
            for tv, base in ((t_own, 2 * c), (t_oth, 2 * (1 - c))):
                for al in range(tv.shape[0]):
                    a = base + al
                    q = None
                    for t in range(tv.shape[2]):
                        v = src[pos_ref[a, j, t]]
                        p = jnp.dot(tv[al, jj, t], v, precision=lax.Precision.HIGHEST,
                                    preferred_element_type=jnp.float32)
                        q = p if q is None else q + p
                    best = q if best is None else jnp.maximum(best, q)
            dst[own_pos + jj] = jnp.where(tgt_ref[j] == 1, jnp.float32(1.0), best)
            return carry

        lax.fori_loop(0, half, block, 0)
        to_partner = pltpu.make_async_remote_copy(
            src_ref=dst.at[pl.ds(own_pos, half)], dst_ref=dst.at[pl.ds(own_pos, half)],
            send_sem=send_sem.at[slot, 0], recv_sem=recv_sem.at[slot, 0],
            device_id=partner, device_id_type=MESH)
        to_neighbour = pltpu.make_async_remote_copy(
            src_ref=dst.at[pl.ds(own_pos, half)], dst_ref=dst.at[pl.ds(nb_halo_pos, half)],
            send_sem=send_sem.at[slot, 1], recv_sem=recv_sem.at[slot, 1],
            device_id=neighbour, device_id_type=MESH)
        to_partner.start()
        to_neighbour.start()
        to_partner.wait_send()
        to_neighbour.wait_send()
        to_partner.wait_recv()
        to_neighbour.wait_recv()

    def pair(k, carry):
        sweep(win0, win1, 1)
        sweep(win1, win0, 0)
        return carry

    lax.fori_loop(0, SWEEPS // 2, pair, 0)
    out_ref[...] = win0[pl.ds(half, 2 * half)]


def per_device(transitions, columns, targets):
    n_states = lax.axis_size("states")
    rb = transitions.shape[1]
    tile = transitions.shape[3]
    ksets = targets.shape[1]
    total_blocks = rb * n_states
    first = lax.axis_index("states") * rb - REACH
    pos = lax.rem(columns - first + 2 * total_blocks, total_blocks).astype(jnp.int32)
    tgt = targets.reshape(rb, tile, ksets)
    half = rb // 2
    out = pl.pallas_call(
        functools.partial(sweep_kernel, n_states),
        out_shape=jax.ShapeDtypeStruct((rb, tile, ksets), jnp.float32),
        in_specs=[
            pl.BlockSpec(memory_space=pltpu.SMEM),
            pl.BlockSpec(memory_space=pl.ANY),
            pl.BlockSpec(memory_space=pltpu.VMEM),
        ],
        out_specs=pl.BlockSpec(memory_space=pltpu.VMEM),
        scratch_shapes=[
            pltpu.VMEM((rb + 2 * REACH, tile, ksets), jnp.float32),
            pltpu.VMEM((rb + 2 * REACH, tile, ksets), jnp.float32),
            pltpu.VMEM((transitions.shape[0], half) + transitions.shape[2:], jnp.float32),
            pltpu.VMEM((transitions.shape[0], half) + transitions.shape[2:], jnp.float32),
            pltpu.SemaphoreType.DMA((3,)),
            pltpu.SemaphoreType.DMA((2, 2)),
            pltpu.SemaphoreType.DMA((2, 2)),
        ],
        compiler_params=pltpu.CompilerParams(
            collective_id=0, has_side_effects=True, vmem_limit_bytes=48 * 1024 * 1024),
    )(pos, transitions, tgt)
    return out.reshape(rb * tile, ksets)


def solution(mesh):
    return jax.shard_map(
        per_device,
        mesh=mesh,
        in_specs=(P("act", "states", None, None, None), P(None, "states", None), P("states", None)),
        out_specs=P("states", None),
        check_vma=False,
    )
```

```python
import functools

import jax
import jax.numpy as jnp
from jax import lax
from jax.experimental import pallas as pl
from jax.experimental.pallas import tpu as pltpu
from jax.sharding import PartitionSpec as P

REACH = 8
SWEEPS = 12
MESH = pl.DeviceIdType.MESH


def split_blocks(src, hi, lo, first, count):
    def body(k, carry):
        v = src[first + k]
        h = v.astype(jnp.bfloat16)
        hi[first + k] = h
        lo[first + k] = (v - h.astype(jnp.float32)).astype(jnp.bfloat16)
        return carry

    lax.fori_loop(0, count, body, 0)


def sweep_kernel(n_states, pos_ref, trans_hbm, tgt_ref, out_ref,
                 win0, win1, hi0, hi1, lo0, lo1, t_own, t_oth, thi, tlo,
                 tsem, send_sem, recv_sem):
    i = lax.axis_index("states")
    c = lax.axis_index("act")
    acts = t_own.shape[0]
    half = t_own.shape[1]
    tile = t_own.shape[3]
    own_pos = half + half * c
    part_pos = 2 * half - half * c
    halo_pos = 3 * half * c
    nb_halo_pos = 3 * half * (1 - c)
    partner = (i, 1 - c)
    neighbour = (lax.rem(i + 2 * c - 1 + n_states, n_states), 1 - c)

    barrier = pltpu.get_barrier_semaphore()
    for dev in (partner, neighbour):
        pl.semaphore_signal(barrier, inc=1, device_id=dev, device_id_type=MESH)
    pl.semaphore_wait(barrier, 2)

    own_copy = pltpu.make_async_copy(trans_hbm.at[:, pl.ds(half * c, half)], t_own, tsem.at[0])
    own_copy.start()
    oth_copy = pltpu.make_async_remote_copy(
        src_ref=trans_hbm.at[:, pl.ds(half * (1 - c), half)], dst_ref=t_oth,
        send_sem=tsem.at[1], recv_sem=tsem.at[2], device_id=partner, device_id_type=MESH)
    oth_copy.start()

    win0[pl.ds(half, 2 * half)] = tgt_ref[...].astype(jnp.float32)
    init = pltpu.make_async_remote_copy(
        src_ref=win0.at[pl.ds(own_pos, half)], dst_ref=win0.at[pl.ds(nb_halo_pos, half)],
        send_sem=send_sem.at[0, 1], recv_sem=recv_sem.at[0, 1],
        device_id=neighbour, device_id_type=MESH)
    init.start()
    split_blocks(win0, hi0, lo0, half, 2 * half)

    def prep(tv, first):
        def body(k, carry):
            al = k // half
            jj = k % half
            for t in range(tv.shape[2]):
                v = tv[al, jj, t]
                h = v.astype(jnp.bfloat16)
                thi[first + al, jj, :, pl.ds(t * tile, tile)] = h
                tlo[first + al, jj, :, pl.ds(t * tile, tile)] = (
                    v - h.astype(jnp.float32)).astype(jnp.bfloat16)
            return carry

        lax.fori_loop(0, acts * half, body, 0)

    own_copy.wait()
    prep(t_own, 0)
    oth_copy.wait_send()
    oth_copy.wait_recv()
    prep(t_oth, acts)
    init.wait_send()
    init.wait_recv()
    split_blocks(win0, hi0, lo0, halo_pos, half)

    def sweep(src_hi, src_lo, dst, dst_hi, dst_lo, slot):
        def block(jj, carry):
            j = half * c + jj
            best = None
            for ab in range(2 * acts):
                a = lax.rem(2 * c + ab, 2 * acts)
                p0 = pos_ref[a, j, 0]
                p1 = pos_ref[a, j, 1]
                vh = jnp.concatenate([src_hi[p0], src_hi[p1]], axis=0)
                vl = jnp.concatenate([src_lo[p0], src_lo[p1]], axis=0)
                th = thi[ab, jj]
                tl = tlo[ab, jj]
                q = jnp.dot(th, vh, preferred_element_type=jnp.float32)
                q = q + jnp.dot(th, vl, preferred_element_type=jnp.float32)
                q = q + jnp.dot(tl, vh, preferred_element_type=jnp.float32)
                best = q if best is None else jnp.maximum(best, q)
            val = jnp.where(tgt_ref[j] == 1, jnp.float32(1.0), best)
            dst[own_pos + jj] = val
            h = val.astype(jnp.bfloat16)
            dst_hi[own_pos + jj] = h
            dst_lo[own_pos + jj] = (val - h.astype(jnp.float32)).astype(jnp.bfloat16)
            pltpu.make_async_remote_copy(
                src_ref=dst.at[own_pos + jj], dst_ref=dst.at[own_pos + jj],
                send_sem=send_sem.at[slot, 0], recv_sem=recv_sem.at[slot, 0],
                device_id=partner, device_id_type=MESH).start()
            pltpu.make_async_remote_copy(
                src_ref=dst.at[own_pos + jj], dst_ref=dst.at[nb_halo_pos + jj],
                send_sem=send_sem.at[slot, 1], recv_sem=recv_sem.at[slot, 1],
                device_id=neighbour, device_id_type=MESH).start()
            return carry

        lax.fori_loop(0, half, block, 0)
        to_partner = pltpu.make_async_remote_copy(
            src_ref=dst.at[pl.ds(own_pos, half)], dst_ref=dst.at[pl.ds(own_pos, half)],
            send_sem=send_sem.at[slot, 0], recv_sem=recv_sem.at[slot, 0],
            device_id=partner, device_id_type=MESH)
        to_neighbour = pltpu.make_async_remote_copy(
            src_ref=dst.at[pl.ds(own_pos, half)], dst_ref=dst.at[pl.ds(nb_halo_pos, half)],
            send_sem=send_sem.at[slot, 1], recv_sem=recv_sem.at[slot, 1],
            device_id=neighbour, device_id_type=MESH)
        to_partner.wait_send()
        to_neighbour.wait_send()
        to_partner.wait_recv()
        split_blocks(dst, dst_hi, dst_lo, part_pos, half)
        to_neighbour.wait_recv()
        split_blocks(dst, dst_hi, dst_lo, halo_pos, half)

    def pair(k, carry):
        sweep(hi0, lo0, win1, hi1, lo1, 1)
        sweep(hi1, lo1, win0, hi0, lo0, 0)
        return carry

    lax.fori_loop(0, SWEEPS // 2, pair, 0)
    out_ref[...] = win0[pl.ds(half, 2 * half)]


def per_device(transitions, columns, targets):
    n_states = lax.axis_size("states")
    rb = transitions.shape[1]
    tile = transitions.shape[3]
    ksets = targets.shape[1]
    total_blocks = rb * n_states
    first = lax.axis_index("states") * rb - REACH
    pos = lax.rem(columns - first + 2 * total_blocks, total_blocks).astype(jnp.int32)
    tgt = targets.reshape(rb, tile, ksets)
    half = rb // 2
    out = pl.pallas_call(
        functools.partial(sweep_kernel, n_states),
        out_shape=jax.ShapeDtypeStruct((rb, tile, ksets), jnp.float32),
        in_specs=[
            pl.BlockSpec(memory_space=pltpu.SMEM),
            pl.BlockSpec(memory_space=pl.ANY),
            pl.BlockSpec(memory_space=pltpu.VMEM),
        ],
        out_specs=pl.BlockSpec(memory_space=pltpu.VMEM),
        scratch_shapes=[
            pltpu.VMEM((rb + 2 * REACH, tile, ksets), jnp.float32),
            pltpu.VMEM((rb + 2 * REACH, tile, ksets), jnp.float32),
            pltpu.VMEM((rb + 2 * REACH, tile, ksets), jnp.bfloat16),
            pltpu.VMEM((rb + 2 * REACH, tile, ksets), jnp.bfloat16),
            pltpu.VMEM((rb + 2 * REACH, tile, ksets), jnp.bfloat16),
            pltpu.VMEM((rb + 2 * REACH, tile, ksets), jnp.bfloat16),
            pltpu.VMEM((transitions.shape[0], half) + transitions.shape[2:], jnp.float32),
            pltpu.VMEM((transitions.shape[0], half) + transitions.shape[2:], jnp.float32),
            pltpu.VMEM((2 * transitions.shape[0], half, tile, 2 * tile), jnp.bfloat16),
            pltpu.VMEM((2 * transitions.shape[0], half, tile, 2 * tile), jnp.bfloat16),
            pltpu.SemaphoreType.DMA((3,)),
            pltpu.SemaphoreType.DMA((2, 2)),
            pltpu.SemaphoreType.DMA((2, 2)),
        ],
        compiler_params=pltpu.CompilerParams(
            collective_id=0, has_side_effects=True, vmem_limit_bytes=48 * 1024 * 1024),
    )(pos, transitions, tgt)
    return out.reshape(rb * tile, ksets)


def solution(mesh):
    return jax.shard_map(
        per_device,
        mesh=mesh,
        in_specs=(P("act", "states", None, None, None), P(None, "states", None), P("states", None)),
        out_specs=P("states", None),
        check_vma=False,
    )
```

```python
import functools

import jax
import jax.numpy as jnp
from jax import lax
from jax.experimental import pallas as pl
from jax.experimental.pallas import tpu as pltpu
from jax.sharding import PartitionSpec as P

REACH = 8
SWEEPS = 12
MESH = pl.DeviceIdType.MESH


def split_blocks(src, hi, lo, first, count):
    def body(k, carry):
        v = src[first + k]
        h = v.astype(jnp.bfloat16)
        hi[first + k] = h
        lo[first + k] = (v - h.astype(jnp.float32)).astype(jnp.bfloat16)
        return carry

    lax.fori_loop(0, count, body, 0)


def sweep_kernel(n_states, pos_ref, trans_hbm, tgt_ref, out_ref,
                 win0, win1, hi0, hi1, lo0, lo1, t_own, t_oth, thi, tlo,
                 tsem, send_sem, recv_sem):
    i = lax.axis_index("states")
    c = lax.axis_index("act")
    acts = t_own.shape[0]
    half = t_own.shape[1]
    tile = t_own.shape[3]
    own_pos = half + half * c
    part_pos = 2 * half - half * c
    halo_pos = 3 * half * c
    nb_halo_pos = 3 * half * (1 - c)
    partner = (i, 1 - c)
    neighbour = (lax.rem(i + 2 * c - 1 + n_states, n_states), 1 - c)

    barrier = pltpu.get_barrier_semaphore()
    for dev in (partner, neighbour):
        pl.semaphore_signal(barrier, inc=1, device_id=dev, device_id_type=MESH)
    pl.semaphore_wait(barrier, 2)

    own_copy = pltpu.make_async_copy(trans_hbm.at[:, pl.ds(half * c, half)], t_own, tsem.at[0])
    own_copy.start()
    oth_copy = pltpu.make_async_remote_copy(
        src_ref=trans_hbm.at[:, pl.ds(half * (1 - c), half)], dst_ref=t_oth,
        send_sem=tsem.at[1], recv_sem=tsem.at[2], device_id=partner, device_id_type=MESH)
    oth_copy.start()

    win0[pl.ds(half, 2 * half)] = tgt_ref[...].astype(jnp.float32)
    init = pltpu.make_async_remote_copy(
        src_ref=win0.at[pl.ds(own_pos, half)], dst_ref=win0.at[pl.ds(nb_halo_pos, half)],
        send_sem=send_sem.at[0, 1], recv_sem=recv_sem.at[0, 1],
        device_id=neighbour, device_id_type=MESH)
    init.start()
    split_blocks(win0, hi0, lo0, half, 2 * half)

    def prep(tv, first):
        def body(k, carry):
            al = k // half
            jj = k % half
            for t in range(tv.shape[2]):
                v = tv[al, jj, t]
                h = v.astype(jnp.bfloat16)
                thi[first + al, jj, :, pl.ds(t * tile, tile)] = h
                tlo[first + al, jj, :, pl.ds(t * tile, tile)] = (
                    v - h.astype(jnp.float32)).astype(jnp.bfloat16)
            return carry

        lax.fori_loop(0, acts * half, body, 0)

    own_copy.wait()
    prep(t_own, 0)
    oth_copy.wait_send()
    oth_copy.wait_recv()
    prep(t_oth, acts)
    init.wait_send()
    init.wait_recv()
    split_blocks(win0, hi0, lo0, halo_pos, half)

    def sweep(src_hi, src_lo, dst, dst_hi, dst_lo, slot, halo=True):
        def block(jj, carry):
            j = half * c + jj
            best = None
            for ab in range(2 * acts):
                a = lax.rem(2 * c + ab, 2 * acts)
                p0 = pos_ref[a, j, 0]
                p1 = pos_ref[a, j, 1]
                vh = jnp.concatenate([src_hi[p0], src_hi[p1]], axis=0)
                vl = jnp.concatenate([src_lo[p0], src_lo[p1]], axis=0)
                th = thi[ab, jj]
                tl = tlo[ab, jj]
                q = jnp.dot(th, vh, preferred_element_type=jnp.float32)
                q = q + jnp.dot(th, vl, preferred_element_type=jnp.float32)
                q = q + jnp.dot(tl, vh, preferred_element_type=jnp.float32)
                best = q if best is None else jnp.maximum(best, q)
            val = jnp.where(tgt_ref[j] == 1, jnp.float32(1.0), best)
            dst[own_pos + jj] = val
            h = val.astype(jnp.bfloat16)
            dst_hi[own_pos + jj] = h
            dst_lo[own_pos + jj] = (val - h.astype(jnp.float32)).astype(jnp.bfloat16)
            pltpu.make_async_remote_copy(
                src_ref=dst.at[own_pos + jj], dst_ref=dst.at[own_pos + jj],
                send_sem=send_sem.at[slot, 0], recv_sem=recv_sem.at[slot, 0],
                device_id=partner, device_id_type=MESH).start()
            if halo:
                pltpu.make_async_remote_copy(
                    src_ref=dst.at[own_pos + jj], dst_ref=dst.at[nb_halo_pos + jj],
                    send_sem=send_sem.at[slot, 1], recv_sem=recv_sem.at[slot, 1],
                    device_id=neighbour, device_id_type=MESH).start()
            return carry

        lax.fori_loop(0, half, block, 0)
        to_partner = pltpu.make_async_remote_copy(
            src_ref=dst.at[pl.ds(own_pos, half)], dst_ref=dst.at[pl.ds(own_pos, half)],
            send_sem=send_sem.at[slot, 0], recv_sem=recv_sem.at[slot, 0],
            device_id=partner, device_id_type=MESH)
        to_neighbour = pltpu.make_async_remote_copy(
            src_ref=dst.at[pl.ds(own_pos, half)], dst_ref=dst.at[pl.ds(nb_halo_pos, half)],
            send_sem=send_sem.at[slot, 1], recv_sem=recv_sem.at[slot, 1],
            device_id=neighbour, device_id_type=MESH)
        to_partner.wait_send()
        to_partner.wait_recv()
        if not halo:
            return
        to_neighbour.wait_send()
        split_blocks(dst, dst_hi, dst_lo, part_pos, half)
        to_neighbour.wait_recv()
        split_blocks(dst, dst_hi, dst_lo, halo_pos, half)

    def pair(k, carry):
        sweep(hi0, lo0, win1, hi1, lo1, 1)
        sweep(hi1, lo1, win0, hi0, lo0, 0)
        return carry

    lax.fori_loop(0, SWEEPS // 2 - 1, pair, 0)
    sweep(hi0, lo0, win1, hi1, lo1, 1)
    sweep(hi1, lo1, win0, hi0, lo0, 0, halo=False)
    out_ref[...] = win0[pl.ds(half, 2 * half)]


def per_device(transitions, columns, targets):
    n_states = lax.axis_size("states")
    rb = transitions.shape[1]
    tile = transitions.shape[3]
    ksets = targets.shape[1]
    total_blocks = rb * n_states
    first = lax.axis_index("states") * rb - REACH
    pos = lax.rem(columns - first + 2 * total_blocks, total_blocks).astype(jnp.int32)
    tgt = targets.reshape(rb, tile, ksets)
    half = rb // 2
    out = pl.pallas_call(
        functools.partial(sweep_kernel, n_states),
        out_shape=jax.ShapeDtypeStruct((rb, tile, ksets), jnp.float32),
        in_specs=[
            pl.BlockSpec(memory_space=pltpu.SMEM),
            pl.BlockSpec(memory_space=pl.ANY),
            pl.BlockSpec(memory_space=pltpu.VMEM),
        ],
        out_specs=pl.BlockSpec(memory_space=pltpu.VMEM),
        scratch_shapes=[
            pltpu.VMEM((rb + 2 * REACH, tile, ksets), jnp.float32),
            pltpu.VMEM((rb + 2 * REACH, tile, ksets), jnp.float32),
            pltpu.VMEM((rb + 2 * REACH, tile, ksets), jnp.bfloat16),
            pltpu.VMEM((rb + 2 * REACH, tile, ksets), jnp.bfloat16),
            pltpu.VMEM((rb + 2 * REACH, tile, ksets), jnp.bfloat16),
            pltpu.VMEM((rb + 2 * REACH, tile, ksets), jnp.bfloat16),
            pltpu.VMEM((transitions.shape[0], half) + transitions.shape[2:], jnp.float32),
            pltpu.VMEM((transitions.shape[0], half) + transitions.shape[2:], jnp.float32),
            pltpu.VMEM((2 * transitions.shape[0], half, tile, 2 * tile), jnp.bfloat16),
            pltpu.VMEM((2 * transitions.shape[0], half, tile, 2 * tile), jnp.bfloat16),
            pltpu.SemaphoreType.DMA((3,)),
            pltpu.SemaphoreType.DMA((2, 2)),
            pltpu.SemaphoreType.DMA((2, 2)),
        ],
        compiler_params=pltpu.CompilerParams(
            collective_id=0, has_side_effects=True, vmem_limit_bytes=48 * 1024 * 1024),
    )(pos, transitions, tgt)
    return out.reshape(rb * tile, ksets)


def solution(mesh):
    return jax.shard_map(
        per_device,
        mesh=mesh,
        in_specs=(P("act", "states", None, None, None), P(None, "states", None), P("states", None)),
        out_specs=P("states", None),
        check_vma=False,
    )
```

```python
import functools

import jax
import jax.numpy as jnp
from jax import lax
from jax.experimental import pallas as pl
from jax.experimental.pallas import tpu as pltpu
from jax.sharding import PartitionSpec as P

REACH = 8
SWEEPS = 12
HALVES = 2
MESH = pl.DeviceIdType.MESH


def split_blocks(src, hi, lo, h, first, count):
    def body(k, carry):
        v = src[h, first + k]
        b = v.astype(jnp.bfloat16)
        hi[h, first + k] = b
        lo[h, first + k] = (v - b.astype(jnp.float32)).astype(jnp.bfloat16)
        return carry

    lax.fori_loop(0, count, body, 0)


def sweep_kernel(n_states, pos_ref, trans_hbm, tgt_ref, out_ref,
                 win0, win1, hi0, hi1, lo0, lo1, t_own, t_oth, thi, tlo,
                 tsem, send_sem, recv_sem):
    i = lax.axis_index("states")
    c = lax.axis_index("act")
    acts = t_own.shape[0]
    half = t_own.shape[1]
    tile = t_own.shape[3]
    own_pos = half + half * c
    part_pos = 2 * half - half * c
    halo_pos = 3 * half * c
    nb_halo_pos = 3 * half * (1 - c)
    partner = (i, 1 - c)
    neighbour = (lax.rem(i + 2 * c - 1 + n_states, n_states), 1 - c)
    wins = (win0, win1)
    his = (hi0, hi1)
    los = (lo0, lo1)

    barrier = pltpu.get_barrier_semaphore()
    for dev in (partner, neighbour):
        pl.semaphore_signal(barrier, inc=1, device_id=dev, device_id_type=MESH)
    pl.semaphore_wait(barrier, 2)

    def copy_to(slot, h, k, start, count, dst_start):
        dev = partner if k == 0 else neighbour
        return pltpu.make_async_remote_copy(
            src_ref=wins[slot].at[h, pl.ds(start, count)],
            dst_ref=wins[slot].at[h, pl.ds(dst_start, count)],
            send_sem=send_sem.at[slot, h, k], recv_sem=recv_sem.at[slot, h, k],
            device_id=dev, device_id_type=MESH)

    for h in range(HALVES):
        win0[h, pl.ds(half, 2 * half)] = tgt_ref[h].astype(jnp.float32)
        copy_to(0, h, 1, own_pos, half, nb_halo_pos).start()

    own_copy = pltpu.make_async_copy(trans_hbm.at[:, pl.ds(half * c, half)], t_own, tsem.at[0])
    own_copy.start()
    oth_copy = pltpu.make_async_remote_copy(
        src_ref=trans_hbm.at[:, pl.ds(half * (1 - c), half)], dst_ref=t_oth,
        send_sem=tsem.at[1], recv_sem=tsem.at[2], device_id=partner, device_id_type=MESH)
    oth_copy.start()
    for h in range(HALVES):
        split_blocks(win0, hi0, lo0, h, half, 2 * half)

    def prep(tv, first):
        def body(k, carry):
            al = k // half
            jj = k % half
            for t in range(tv.shape[2]):
                v = tv[al, jj, t]
                b = v.astype(jnp.bfloat16)
                thi[first + al, jj, :, pl.ds(t * tile, tile)] = b
                tlo[first + al, jj, :, pl.ds(t * tile, tile)] = (
                    v - b.astype(jnp.float32)).astype(jnp.bfloat16)
            return carry

        lax.fori_loop(0, acts * half, body, 0)

    own_copy.wait()
    prep(t_own, 0)
    oth_copy.wait_send()
    oth_copy.wait_recv()
    prep(t_oth, acts)

    def stage(h, src, dst, first=False, halo=True):
        if first:
            done = copy_to(src, h, 1, own_pos, half, halo_pos)
            done.wait_send()
            done.wait_recv()
            split_blocks(wins[src], his[src], los[src], h, halo_pos, half)
        else:
            for k, start in ((0, part_pos), (1, halo_pos)):
                done = copy_to(src, h, k, own_pos, half, start)
                done.wait_send()
                done.wait_recv()
                split_blocks(wins[src], his[src], los[src], h, start, half)
        src_hi, src_lo = his[src], los[src]
        dst_win, dst_hi, dst_lo = wins[dst], his[dst], los[dst]

        def block(jj, carry):
            j = half * c + jj
            best = None
            for ab in range(2 * acts):
                a = lax.rem(2 * c + ab, 2 * acts)
                p0 = pos_ref[a, j, 0]
                p1 = pos_ref[a, j, 1]
                vh = jnp.concatenate([src_hi[h, p0], src_hi[h, p1]], axis=0)
                vl = jnp.concatenate([src_lo[h, p0], src_lo[h, p1]], axis=0)
                th = thi[ab, jj]
                tl = tlo[ab, jj]
                q = jnp.dot(th, vh, preferred_element_type=jnp.float32)
                q = q + jnp.dot(th, vl, preferred_element_type=jnp.float32)
                q = q + jnp.dot(tl, vh, preferred_element_type=jnp.float32)
                best = q if best is None else jnp.maximum(best, q)
            val = jnp.where(tgt_ref[h, j] == 1, jnp.float32(1.0), best)
            dst_win[h, own_pos + jj] = val
            b = val.astype(jnp.bfloat16)
            dst_hi[h, own_pos + jj] = b
            dst_lo[h, own_pos + jj] = (val - b.astype(jnp.float32)).astype(jnp.bfloat16)
            copy_to(dst, h, 0, own_pos + jj, 1, own_pos + jj).start()
            if halo:
                copy_to(dst, h, 1, own_pos + jj, 1, nb_halo_pos + jj).start()
            return carry

        lax.fori_loop(0, half, block, 0)

    for h in range(HALVES):
        stage(h, 0, 1, first=True)

    def pair(k, carry):
        for h in range(HALVES):
            stage(h, 1, 0)
        for h in range(HALVES):
            stage(h, 0, 1)
        return carry

    lax.fori_loop(0, SWEEPS // 2 - 1, pair, 0)
    for h in range(HALVES):
        stage(h, 1, 0, halo=False)
    for h in range(HALVES):
        done = copy_to(0, h, 0, own_pos, half, part_pos)
        done.wait_send()
        done.wait_recv()
        out_ref[h] = win0[h, pl.ds(half, 2 * half)]


def per_device(transitions, columns, targets):
    n_states = lax.axis_size("states")
    rb = transitions.shape[1]
    tile = transitions.shape[3]
    ksets = targets.shape[1]
    kh = ksets // HALVES
    total_blocks = rb * n_states
    first = lax.axis_index("states") * rb - REACH
    pos = lax.rem(columns - first + 2 * total_blocks, total_blocks).astype(jnp.int32)
    tgt = targets.reshape(rb, tile, HALVES, kh).transpose(2, 0, 1, 3)
    half = rb // 2
    wshape = (HALVES, rb + 2 * REACH, tile, kh)
    out = pl.pallas_call(
        functools.partial(sweep_kernel, n_states),
        out_shape=jax.ShapeDtypeStruct((HALVES, rb, tile, kh), jnp.float32),
        in_specs=[
            pl.BlockSpec(memory_space=pltpu.SMEM),
            pl.BlockSpec(memory_space=pl.ANY),
            pl.BlockSpec(memory_space=pltpu.VMEM),
        ],
        out_specs=pl.BlockSpec(memory_space=pltpu.VMEM),
        scratch_shapes=[
            pltpu.VMEM(wshape, jnp.float32),
            pltpu.VMEM(wshape, jnp.float32),
            pltpu.VMEM(wshape, jnp.bfloat16),
            pltpu.VMEM(wshape, jnp.bfloat16),
            pltpu.VMEM(wshape, jnp.bfloat16),
            pltpu.VMEM(wshape, jnp.bfloat16),
            pltpu.VMEM((transitions.shape[0], half) + transitions.shape[2:], jnp.float32),
            pltpu.VMEM((transitions.shape[0], half) + transitions.shape[2:], jnp.float32),
            pltpu.VMEM((2 * transitions.shape[0], half, tile, 2 * tile), jnp.bfloat16),
            pltpu.VMEM((2 * transitions.shape[0], half, tile, 2 * tile), jnp.bfloat16),
            pltpu.SemaphoreType.DMA((3,)),
            pltpu.SemaphoreType.DMA((2, HALVES, 2)),
            pltpu.SemaphoreType.DMA((2, HALVES, 2)),
        ],
        compiler_params=pltpu.CompilerParams(
            collective_id=0, has_side_effects=True, vmem_limit_bytes=60 * 1024 * 1024),
    )(pos, transitions, tgt)
    return out.transpose(1, 2, 0, 3).reshape(rb * tile, ksets)


def solution(mesh):
    return jax.shard_map(
        per_device,
        mesh=mesh,
        in_specs=(P("act", "states", None, None, None), P(None, "states", None), P("states", None)),
        out_specs=P("states", None),
        check_vma=False,
    )
```

```python
import functools

import jax
import jax.numpy as jnp
from jax import lax
from jax.experimental import pallas as pl
from jax.experimental.pallas import tpu as pltpu
from jax.sharding import PartitionSpec as P

REACH = 8
SWEEPS = 12
HALVES = 2
MESH = pl.DeviceIdType.MESH


def split_blocks(src, hi, lo, h, first, count):
    def body(k, carry):
        v = src[h, first + k]
        b = v.astype(jnp.bfloat16)
        hi[h, first + k] = b
        lo[h, first + k] = (v - b.astype(jnp.float32)).astype(jnp.bfloat16)
        return carry

    lax.fori_loop(0, count, body, 0)


def sweep_kernel(n_states, pos_ref, trans_hbm, tgt_ref, out_ref,
                 win0, win1, hi0, hi1, lo0, lo1, t_own, t_oth, thi, tlo,
                 tsem, send_sem, recv_sem):
    i = lax.axis_index("states")
    c = lax.axis_index("act")
    acts = t_own.shape[0]
    half = t_own.shape[1]
    tile = t_own.shape[3]
    own_pos = half + half * c
    part_pos = 2 * half - half * c
    halo_pos = 3 * half * c
    nb_halo_pos = 3 * half * (1 - c)
    partner = (i, 1 - c)
    neighbour = (lax.rem(i + 2 * c - 1 + n_states, n_states), 1 - c)
    wins = (win0, win1)
    his = (hi0, hi1)
    los = (lo0, lo1)

    barrier = pltpu.get_barrier_semaphore()
    for dev in (partner, neighbour):
        pl.semaphore_signal(barrier, inc=1, device_id=dev, device_id_type=MESH)
    pl.semaphore_wait(barrier, 2)

    def copy_to(slot, h, k, start, count, dst_start):
        dev = partner if k == 0 else neighbour
        return pltpu.make_async_remote_copy(
            src_ref=wins[slot].at[h, pl.ds(start, count)],
            dst_ref=wins[slot].at[h, pl.ds(dst_start, count)],
            send_sem=send_sem.at[slot, h, k], recv_sem=recv_sem.at[slot, h, k],
            device_id=dev, device_id_type=MESH)

    for h in range(HALVES):
        win0[h, pl.ds(half, 2 * half)] = tgt_ref[h].astype(jnp.float32)
        copy_to(0, h, 1, own_pos, half, nb_halo_pos).start()

    own_copy = pltpu.make_async_copy(trans_hbm.at[:, pl.ds(half * c, half)], t_own, tsem.at[0])
    own_copy.start()
    oth_copy = pltpu.make_async_remote_copy(
        src_ref=trans_hbm.at[:, pl.ds(half * (1 - c), half)], dst_ref=t_oth,
        send_sem=tsem.at[1], recv_sem=tsem.at[2], device_id=partner, device_id_type=MESH)
    oth_copy.start()
    for h in range(HALVES):
        split_blocks(win0, hi0, lo0, h, half, 2 * half)

    def prep(tv, first):
        def body(k, carry):
            al = k // half
            jj = k % half
            for t in range(tv.shape[2]):
                v = tv[al, jj, t]
                b = v.astype(jnp.bfloat16)
                thi[first + al, jj, pl.ds(t * tile, tile), :] = b
                tlo[first + al, jj, pl.ds(t * tile, tile), :] = (
                    v - b.astype(jnp.float32)).astype(jnp.bfloat16)
            return carry

        lax.fori_loop(0, acts * half, body, 0)

    own_copy.wait()
    prep(t_own, 0)
    oth_copy.wait_send()
    oth_copy.wait_recv()
    prep(t_oth, acts)

    def stage(h, src, dst, first=False, halo=True):
        if first:
            done = copy_to(src, h, 1, own_pos, half, halo_pos)
            done.wait_send()
            done.wait_recv()
            split_blocks(wins[src], his[src], los[src], h, halo_pos, half)
        else:
            for k, start in ((0, part_pos), (1, halo_pos)):
                done = copy_to(src, h, k, own_pos, half, start)
                done.wait_send()
                done.wait_recv()
                split_blocks(wins[src], his[src], los[src], h, start, half)
        src_hi, src_lo = his[src], los[src]
        dst_win, dst_hi, dst_lo = wins[dst], his[dst], los[dst]

        def block(jj, carry):
            j = half * c + jj
            best = None
            for ab in range(2 * acts):
                a = lax.rem(2 * c + ab, 2 * acts)
                p0 = pos_ref[a, j, 0]
                p1 = pos_ref[a, j, 1]
                vh = jnp.concatenate([src_hi[h, p0], src_hi[h, p1]], axis=1)
                vl = jnp.concatenate([src_lo[h, p0], src_lo[h, p1]], axis=1)
                th = thi[ab, jj]
                tl = tlo[ab, jj]
                q = jnp.dot(vh, th, preferred_element_type=jnp.float32)
                q = q + jnp.dot(vl, th, preferred_element_type=jnp.float32)
                q = q + jnp.dot(vh, tl, preferred_element_type=jnp.float32)
                best = q if best is None else jnp.maximum(best, q)
            val = jnp.where(tgt_ref[h, j] == 1, jnp.float32(1.0), best)
            dst_win[h, own_pos + jj] = val
            b = val.astype(jnp.bfloat16)
            dst_hi[h, own_pos + jj] = b
            dst_lo[h, own_pos + jj] = (val - b.astype(jnp.float32)).astype(jnp.bfloat16)
            copy_to(dst, h, 0, own_pos + jj, 1, own_pos + jj).start()
            if halo:
                copy_to(dst, h, 1, own_pos + jj, 1, nb_halo_pos + jj).start()
            return carry

        lax.fori_loop(0, half, block, 0)

    for h in range(HALVES):
        stage(h, 0, 1, first=True)

    def pair(k, carry):
        for h in range(HALVES):
            stage(h, 1, 0)
        for h in range(HALVES):
            stage(h, 0, 1)
        return carry

    lax.fori_loop(0, SWEEPS // 2 - 1, pair, 0)
    for h in range(HALVES):
        stage(h, 1, 0, halo=False)
    for h in range(HALVES):
        done = copy_to(0, h, 0, own_pos, half, part_pos)
        done.wait_send()
        done.wait_recv()
        out_ref[h] = win0[h, pl.ds(half, 2 * half)]


def per_device(transitions, columns, targets):
    n_states = lax.axis_size("states")
    rb = transitions.shape[1]
    tile = transitions.shape[3]
    ksets = targets.shape[1]
    kh = ksets // HALVES
    total_blocks = rb * n_states
    first = lax.axis_index("states") * rb - REACH
    pos = lax.rem(columns - first + 2 * total_blocks, total_blocks).astype(jnp.int32)
    tgt = targets.reshape(rb, tile, HALVES, kh).transpose(2, 0, 3, 1)
    trans_t = jnp.swapaxes(transitions, -1, -2)
    half = rb // 2
    wshape = (HALVES, rb + 2 * REACH, kh, tile)
    out = pl.pallas_call(
        functools.partial(sweep_kernel, n_states),
        out_shape=jax.ShapeDtypeStruct((HALVES, rb, kh, tile), jnp.float32),
        in_specs=[
            pl.BlockSpec(memory_space=pltpu.SMEM),
            pl.BlockSpec(memory_space=pl.ANY),
            pl.BlockSpec(memory_space=pltpu.VMEM),
        ],
        out_specs=pl.BlockSpec(memory_space=pltpu.VMEM),
        scratch_shapes=[
            pltpu.VMEM(wshape, jnp.float32),
            pltpu.VMEM(wshape, jnp.float32),
            pltpu.VMEM(wshape, jnp.bfloat16),
            pltpu.VMEM(wshape, jnp.bfloat16),
            pltpu.VMEM(wshape, jnp.bfloat16),
            pltpu.VMEM(wshape, jnp.bfloat16),
            pltpu.VMEM((transitions.shape[0], half) + transitions.shape[2:], jnp.float32),
            pltpu.VMEM((transitions.shape[0], half) + transitions.shape[2:], jnp.float32),
            pltpu.VMEM((2 * transitions.shape[0], half, 2 * tile, tile), jnp.bfloat16),
            pltpu.VMEM((2 * transitions.shape[0], half, 2 * tile, tile), jnp.bfloat16),
            pltpu.SemaphoreType.DMA((3,)),
            pltpu.SemaphoreType.DMA((2, HALVES, 2)),
            pltpu.SemaphoreType.DMA((2, HALVES, 2)),
        ],
        compiler_params=pltpu.CompilerParams(
            collective_id=0, has_side_effects=True, vmem_limit_bytes=60 * 1024 * 1024),
    )(pos, trans_t, tgt)
    return out.transpose(1, 3, 0, 2).reshape(rb * tile, ksets)


def solution(mesh):
    return jax.shard_map(
        per_device,
        mesh=mesh,
        in_specs=(P("act", "states", None, None, None), P(None, "states", None), P("states", None)),
        out_specs=P("states", None),
        check_vma=False,
    )
```

```python
import functools

import jax
import jax.numpy as jnp
from jax import lax
from jax.experimental import pallas as pl
from jax.experimental.pallas import tpu as pltpu
from jax.sharding import PartitionSpec as P

REACH = 8
SWEEPS = 12
HALVES = 2
MESH = pl.DeviceIdType.MESH


def split_blocks(src, hi, lo, h, first, count):
    def body(k, carry):
        v = src[h, first + k]
        b = v.astype(jnp.bfloat16)
        hi[h, first + k] = b
        lo[h, first + k] = (v - b.astype(jnp.float32)).astype(jnp.bfloat16)
        return carry

    lax.fori_loop(0, count, body, 0)


def sweep_kernel(n_states, pos_ref, trans_hbm, tgt_in, out_ref,
                 win0, win1, hi0, hi1, lo0, lo1, t_own, t_oth, thi, tlo, tgt_ref,
                 tsem, send_sem, recv_sem):
    i = lax.axis_index("states")
    c = lax.axis_index("act")
    acts = t_own.shape[0]
    half = t_own.shape[1]
    tile = t_own.shape[3]
    own_pos = half + half * c
    part_pos = 2 * half - half * c
    halo_pos = 3 * half * c
    nb_halo_pos = 3 * half * (1 - c)
    partner = (i, 1 - c)
    neighbour = (lax.rem(i + 2 * c - 1 + n_states, n_states), 1 - c)
    wins = (win0, win1)
    his = (hi0, hi1)
    los = (lo0, lo1)

    barrier = pltpu.get_barrier_semaphore()
    for dev in (partner, neighbour):
        pl.semaphore_signal(barrier, inc=1, device_id=dev, device_id_type=MESH)
    pl.semaphore_wait(barrier, 2)

    def copy_to(slot, h, k, start, count, dst_start):
        dev = partner if k == 0 else neighbour
        return pltpu.make_async_remote_copy(
            src_ref=wins[slot].at[h, pl.ds(start, count)],
            dst_ref=wins[slot].at[h, pl.ds(dst_start, count)],
            send_sem=send_sem.at[slot, h, k], recv_sem=recv_sem.at[slot, h, k],
            device_id=dev, device_id_type=MESH)

    kh = win0.shape[2]

    def load_targets(b, carry):
        tf = jnp.transpose(tgt_in[b].astype(jnp.float32))
        for h in range(HALVES):
            part = tf[h * kh:(h + 1) * kh]
            tgt_ref[h, b] = part
            win0[h, half + b] = part
        return carry

    lax.fori_loop(0, 2 * half, load_targets, 0)
    for h in range(HALVES):
        copy_to(0, h, 1, own_pos, half, nb_halo_pos).start()

    own_copy = pltpu.make_async_copy(trans_hbm.at[:, pl.ds(half * c, half)], t_own, tsem.at[0])
    own_copy.start()
    oth_copy = pltpu.make_async_remote_copy(
        src_ref=trans_hbm.at[:, pl.ds(half * (1 - c), half)], dst_ref=t_oth,
        send_sem=tsem.at[1], recv_sem=tsem.at[2], device_id=partner, device_id_type=MESH)
    oth_copy.start()
    for h in range(HALVES):
        split_blocks(win0, hi0, lo0, h, half, 2 * half)

    def prep(tv, first):
        def body(k, carry):
            al = k // half
            jj = k % half
            for t in range(tv.shape[2]):
                v = jnp.transpose(tv[al, jj, t])
                b = v.astype(jnp.bfloat16)
                thi[first + al, jj, pl.ds(t * tile, tile), :] = b
                tlo[first + al, jj, pl.ds(t * tile, tile), :] = (
                    v - b.astype(jnp.float32)).astype(jnp.bfloat16)
            return carry

        lax.fori_loop(0, acts * half, body, 0)

    own_copy.wait()
    prep(t_own, 0)
    oth_copy.wait_send()
    oth_copy.wait_recv()
    prep(t_oth, acts)

    def stage(h, src, dst, first=False, halo=True):
        if first:
            done = copy_to(src, h, 1, own_pos, half, halo_pos)
            done.wait_send()
            done.wait_recv()
            split_blocks(wins[src], his[src], los[src], h, halo_pos, half)
        else:
            for k, start in ((0, part_pos), (1, halo_pos)):
                done = copy_to(src, h, k, own_pos, half, start)
                done.wait_send()
                done.wait_recv()
                split_blocks(wins[src], his[src], los[src], h, start, half)
        src_hi, src_lo = his[src], los[src]
        dst_win, dst_hi, dst_lo = wins[dst], his[dst], los[dst]

        def block(jj, carry):
            j = half * c + jj
            best = None
            for ab in range(2 * acts):
                a = lax.rem(2 * c + ab, 2 * acts)
                p0 = pos_ref[a, j, 0]
                p1 = pos_ref[a, j, 1]
                vh = jnp.concatenate([src_hi[h, p0], src_hi[h, p1]], axis=1)
                vl = jnp.concatenate([src_lo[h, p0], src_lo[h, p1]], axis=1)
                th = thi[ab, jj]
                tl = tlo[ab, jj]
                q = jnp.dot(vh, th, preferred_element_type=jnp.float32)
                q = q + jnp.dot(vl, th, preferred_element_type=jnp.float32)
                q = q + jnp.dot(vh, tl, preferred_element_type=jnp.float32)
                best = q if best is None else jnp.maximum(best, q)
            val = jnp.where(tgt_ref[h, j] == 1.0, jnp.float32(1.0), best)
            dst_win[h, own_pos + jj] = val
            b = val.astype(jnp.bfloat16)
            dst_hi[h, own_pos + jj] = b
            dst_lo[h, own_pos + jj] = (val - b.astype(jnp.float32)).astype(jnp.bfloat16)
            copy_to(dst, h, 0, own_pos + jj, 1, own_pos + jj).start()
            if halo:
                copy_to(dst, h, 1, own_pos + jj, 1, nb_halo_pos + jj).start()
            return carry

        lax.fori_loop(0, half, block, 0)

    for h in range(HALVES):
        stage(h, 0, 1, first=True)

    def pair(k, carry):
        for h in range(HALVES):
            stage(h, 1, 0)
        for h in range(HALVES):
            stage(h, 0, 1)
        return carry

    lax.fori_loop(0, SWEEPS // 2 - 1, pair, 0)
    for h in range(HALVES):
        stage(h, 1, 0, halo=False)
    for h in range(HALVES):
        done = copy_to(0, h, 0, own_pos, half, part_pos)
        done.wait_send()
        done.wait_recv()

    def store_out(b, carry):
        both = jnp.concatenate([win0[h, half + b] for h in range(HALVES)], axis=0)
        out_ref[b] = jnp.transpose(both)
        return carry

    lax.fori_loop(0, 2 * half, store_out, 0)


def per_device(transitions, columns, targets):
    n_states = lax.axis_size("states")
    rb = transitions.shape[1]
    tile = transitions.shape[3]
    ksets = targets.shape[1]
    kh = ksets // HALVES
    total_blocks = rb * n_states
    first = lax.axis_index("states") * rb - REACH
    pos = lax.rem(columns - first + 2 * total_blocks, total_blocks).astype(jnp.int32)
    tgt = targets.reshape(rb, tile, ksets)
    half = rb // 2
    wshape = (HALVES, rb + 2 * REACH, kh, tile)
    out = pl.pallas_call(
        functools.partial(sweep_kernel, n_states),
        out_shape=jax.ShapeDtypeStruct((rb, tile, ksets), jnp.float32),
        in_specs=[
            pl.BlockSpec(memory_space=pltpu.SMEM),
            pl.BlockSpec(memory_space=pl.ANY),
            pl.BlockSpec(memory_space=pltpu.VMEM),
        ],
        out_specs=pl.BlockSpec(memory_space=pltpu.VMEM),
        scratch_shapes=[
            pltpu.VMEM(wshape, jnp.float32),
            pltpu.VMEM(wshape, jnp.float32),
            pltpu.VMEM(wshape, jnp.bfloat16),
            pltpu.VMEM(wshape, jnp.bfloat16),
            pltpu.VMEM(wshape, jnp.bfloat16),
            pltpu.VMEM(wshape, jnp.bfloat16),
            pltpu.VMEM((transitions.shape[0], half) + transitions.shape[2:], jnp.float32),
            pltpu.VMEM((transitions.shape[0], half) + transitions.shape[2:], jnp.float32),
            pltpu.VMEM((2 * transitions.shape[0], half, 2 * tile, tile), jnp.bfloat16),
            pltpu.VMEM((2 * transitions.shape[0], half, 2 * tile, tile), jnp.bfloat16),
            pltpu.VMEM((HALVES, rb, kh, tile), jnp.float32),
            pltpu.SemaphoreType.DMA((3,)),
            pltpu.SemaphoreType.DMA((2, HALVES, 2)),
            pltpu.SemaphoreType.DMA((2, HALVES, 2)),
        ],
        compiler_params=pltpu.CompilerParams(
            collective_id=0, has_side_effects=True, vmem_limit_bytes=60 * 1024 * 1024),
    )(pos, transitions, tgt)
    return out.reshape(rb * tile, ksets)


def solution(mesh):
    return jax.shard_map(
        per_device,
        mesh=mesh,
        in_specs=(P("act", "states", None, None, None), P(None, "states", None), P("states", None)),
        out_specs=P("states", None),
        check_vma=False,
    )
```

```python
import functools

import jax
import jax.numpy as jnp
from jax import lax
from jax.experimental import pallas as pl
from jax.experimental.pallas import tpu as pltpu
from jax.sharding import PartitionSpec as P

REACH = 8
SWEEPS = 12
HALVES = 2
MESH = pl.DeviceIdType.MESH


def split_blocks(src, hi, lo, h, first, count):
    def body(k, carry):
        v = src[h, first + k]
        b = v.astype(jnp.bfloat16)
        hi[h, first + k] = b
        lo[h, first + k] = (v - b.astype(jnp.float32)).astype(jnp.bfloat16)
        return carry

    lax.fori_loop(0, count, body, 0)


def sweep_kernel(n_states, pos_ref, trans_hbm, tgt_in, out_ref,
                 win0, win1, hi0, hi1, lo0, lo1, t_own, t_oth, thi, tlo, tgt_ref,
                 tsem, send_sem, recv_sem):
    i = lax.axis_index("states")
    c = lax.axis_index("act")
    acts = t_own.shape[0]
    half = t_own.shape[1]
    tile = t_own.shape[3]
    own_pos = half + half * c
    part_pos = 2 * half - half * c
    halo_pos = 3 * half * c
    nb_halo_pos = 3 * half * (1 - c)
    partner = (i, 1 - c)
    neighbour = (lax.rem(i + 2 * c - 1 + n_states, n_states), 1 - c)
    fwd_dev = (lax.rem(i + 1 - 2 * c + n_states, n_states), c)
    fwd_src = (lax.rem(i + 2 * c - 1 + n_states, n_states), c)
    wins = (win0, win1)
    his = (hi0, hi1)
    los = (lo0, lo1)

    barrier = pltpu.get_barrier_semaphore()
    for dev in (partner, neighbour, fwd_dev, fwd_src):
        pl.semaphore_signal(barrier, inc=1, device_id=dev, device_id_type=MESH)
    pl.semaphore_wait(barrier, 4)

    def copy_to(slot, h, k, start, count, dst_start, dev=None):
        if dev is None:
            dev = partner if k == 0 else neighbour
        return pltpu.make_async_remote_copy(
            src_ref=wins[slot].at[h, pl.ds(start, count)],
            dst_ref=wins[slot].at[h, pl.ds(dst_start, count)],
            send_sem=send_sem.at[slot, h, k], recv_sem=recv_sem.at[slot, h, k],
            device_id=dev, device_id_type=MESH)

    kh = win0.shape[2]

    def load_targets(b, carry):
        tf = jnp.transpose(tgt_in[b].astype(jnp.float32))
        for h in range(HALVES):
            part = tf[h * kh:(h + 1) * kh]
            tgt_ref[h, b] = part
            win0[h, half + b] = part
        return carry

    lax.fori_loop(0, 2 * half, load_targets, 0)
    for h in range(HALVES):
        copy_to(0, h, 1, own_pos, half, nb_halo_pos).start()

    own_copy = pltpu.make_async_copy(trans_hbm.at[:, pl.ds(half * c, half)], t_own, tsem.at[0])
    own_copy.start()
    oth_copy = pltpu.make_async_remote_copy(
        src_ref=trans_hbm.at[:, pl.ds(half * (1 - c), half)], dst_ref=t_oth,
        send_sem=tsem.at[1], recv_sem=tsem.at[2], device_id=partner, device_id_type=MESH)
    oth_copy.start()
    for h in range(HALVES):
        split_blocks(win0, hi0, lo0, h, half, 2 * half)

    def prep(tv, first):
        def body(k, carry):
            al = k // half
            jj = k % half
            for t in range(tv.shape[2]):
                v = jnp.transpose(tv[al, jj, t])
                b = v.astype(jnp.bfloat16)
                thi[first + al, jj, pl.ds(t * tile, tile), :] = b
                tlo[first + al, jj, pl.ds(t * tile, tile), :] = (
                    v - b.astype(jnp.float32)).astype(jnp.bfloat16)
            return carry

        lax.fori_loop(0, acts * half, body, 0)

    own_copy.wait()
    prep(t_own, 0)
    oth_copy.wait_send()
    oth_copy.wait_recv()
    prep(t_oth, acts)

    def stage(h, src, dst, first=False, halo=True):
        if first:
            done = copy_to(src, h, 1, own_pos, half, halo_pos)
            done.wait_send()
            done.wait_recv()
            split_blocks(wins[src], his[src], los[src], h, halo_pos, half)
        elif h == 0:
            got = copy_to(src, 1, 0, own_pos, half, part_pos)
            got.wait_recv()
            copy_to(src, 1, 1, part_pos, half, halo_pos, dev=fwd_dev).start()
            split_blocks(wins[src], his[src], los[src], 1, part_pos, half)
            for k, start in ((0, part_pos), (1, halo_pos)):
                done = copy_to(src, h, k, own_pos, half, start)
                done.wait_send()
                done.wait_recv()
                split_blocks(wins[src], his[src], los[src], h, start, half)
        else:
            copy_to(src, h, 0, own_pos, half, part_pos).wait_send()
            done = copy_to(src, h, 1, part_pos, half, halo_pos, dev=fwd_dev)
            done.wait_send()
            done.wait_recv()
            split_blocks(wins[src], his[src], los[src], h, halo_pos, half)
        src_hi, src_lo = his[src], los[src]
        dst_win, dst_hi, dst_lo = wins[dst], his[dst], los[dst]

        def block(jj, carry):
            j = half * c + jj
            best = None
            for ab in range(2 * acts):
                a = lax.rem(2 * c + ab, 2 * acts)
                p0 = pos_ref[a, j, 0]
                p1 = pos_ref[a, j, 1]
                vh = jnp.concatenate([src_hi[h, p0], src_hi[h, p1]], axis=1)
                vl = jnp.concatenate([src_lo[h, p0], src_lo[h, p1]], axis=1)
                th = thi[ab, jj]
                tl = tlo[ab, jj]
                q = jnp.dot(vh, th, preferred_element_type=jnp.float32)
                q = q + jnp.dot(vl, th, preferred_element_type=jnp.float32)
                q = q + jnp.dot(vh, tl, preferred_element_type=jnp.float32)
                best = q if best is None else jnp.maximum(best, q)
            val = jnp.where(tgt_ref[h, j] == 1.0, jnp.float32(1.0), best)
            dst_win[h, own_pos + jj] = val
            b = val.astype(jnp.bfloat16)
            dst_hi[h, own_pos + jj] = b
            dst_lo[h, own_pos + jj] = (val - b.astype(jnp.float32)).astype(jnp.bfloat16)
            copy_to(dst, h, 0, own_pos + jj, 1, own_pos + jj).start()
            if halo and h == 0:
                copy_to(dst, h, 1, own_pos + jj, 1, nb_halo_pos + jj).start()
            return carry

        lax.fori_loop(0, half, block, 0)

    for h in range(HALVES):
        stage(h, 0, 1, first=True)

    def pair(k, carry):
        for h in range(HALVES):
            stage(h, 1, 0)
        for h in range(HALVES):
            stage(h, 0, 1)
        return carry

    lax.fori_loop(0, SWEEPS // 2 - 1, pair, 0)
    for h in range(HALVES):
        stage(h, 1, 0, halo=False)
    for h in range(HALVES):
        done = copy_to(0, h, 0, own_pos, half, part_pos)
        done.wait_send()
        done.wait_recv()

    def store_out(b, carry):
        both = jnp.concatenate([win0[h, half + b] for h in range(HALVES)], axis=0)
        out_ref[b] = jnp.transpose(both)
        return carry

    lax.fori_loop(0, 2 * half, store_out, 0)


def per_device(transitions, columns, targets):
    n_states = lax.axis_size("states")
    rb = transitions.shape[1]
    tile = transitions.shape[3]
    ksets = targets.shape[1]
    kh = ksets // HALVES
    total_blocks = rb * n_states
    first = lax.axis_index("states") * rb - REACH
    pos = lax.rem(columns - first + 2 * total_blocks, total_blocks).astype(jnp.int32)
    tgt = targets.reshape(rb, tile, ksets)
    half = rb // 2
    wshape = (HALVES, rb + 2 * REACH, kh, tile)
    out = pl.pallas_call(
        functools.partial(sweep_kernel, n_states),
        out_shape=jax.ShapeDtypeStruct((rb, tile, ksets), jnp.float32),
        in_specs=[
            pl.BlockSpec(memory_space=pltpu.SMEM),
            pl.BlockSpec(memory_space=pl.ANY),
            pl.BlockSpec(memory_space=pltpu.VMEM),
        ],
        out_specs=pl.BlockSpec(memory_space=pltpu.VMEM),
        scratch_shapes=[
            pltpu.VMEM(wshape, jnp.float32),
            pltpu.VMEM(wshape, jnp.float32),
            pltpu.VMEM(wshape, jnp.bfloat16),
            pltpu.VMEM(wshape, jnp.bfloat16),
            pltpu.VMEM(wshape, jnp.bfloat16),
            pltpu.VMEM(wshape, jnp.bfloat16),
            pltpu.VMEM((transitions.shape[0], half) + transitions.shape[2:], jnp.float32),
            pltpu.VMEM((transitions.shape[0], half) + transitions.shape[2:], jnp.float32),
            pltpu.VMEM((2 * transitions.shape[0], half, 2 * tile, tile), jnp.bfloat16),
            pltpu.VMEM((2 * transitions.shape[0], half, 2 * tile, tile), jnp.bfloat16),
            pltpu.VMEM((HALVES, rb, kh, tile), jnp.float32),
            pltpu.SemaphoreType.DMA((3,)),
            pltpu.SemaphoreType.DMA((2, HALVES, 2)),
            pltpu.SemaphoreType.DMA((2, HALVES, 2)),
        ],
        compiler_params=pltpu.CompilerParams(
            collective_id=0, has_side_effects=True, vmem_limit_bytes=60 * 1024 * 1024),
    )(pos, transitions, tgt)
    return out.reshape(rb * tile, ksets)


def solution(mesh):
    return jax.shard_map(
        per_device,
        mesh=mesh,
        in_specs=(P("act", "states", None, None, None), P(None, "states", None), P("states", None)),
        out_specs=P("states", None),
        check_vma=False,
    )
```

```python
import functools

import jax
import jax.numpy as jnp
from jax import lax
from jax.experimental import pallas as pl
from jax.experimental.pallas import tpu as pltpu
from jax.sharding import PartitionSpec as P

REACH = 8
SWEEPS = 12
HALVES = 2
LAG = 2
MESH = pl.DeviceIdType.MESH


def split_blocks(src, hi, lo, h, first, count):
    def body(k, carry):
        v = src[h, first + k]
        b = v.astype(jnp.bfloat16)
        hi[h, first + k] = b
        lo[h, first + k] = (v - b.astype(jnp.float32)).astype(jnp.bfloat16)
        return carry

    lax.fori_loop(0, count, body, 0)


def sweep_kernel(n_states, pos_ref, trans_hbm, tgt_in, out_ref,
                 win0, win1, hi0, hi1, lo0, lo1, t_own, t_oth, thi, tlo, tgt_ref,
                 tsem, send_sem, recv_sem, part_sem):
    i = lax.axis_index("states")
    c = lax.axis_index("act")
    acts = t_own.shape[0]
    half = t_own.shape[1]
    tile = t_own.shape[3]
    own_pos = half + half * c
    part_pos = 2 * half - half * c
    halo_pos = 3 * half * c
    nb_halo_pos = 3 * half * (1 - c)
    partner = (i, 1 - c)
    neighbour = (lax.rem(i + 2 * c - 1 + n_states, n_states), 1 - c)
    fwd_dev = (lax.rem(i + 1 - 2 * c + n_states, n_states), c)
    fwd_src = (lax.rem(i + 2 * c - 1 + n_states, n_states), c)
    wins = (win0, win1)
    his = (hi0, hi1)
    los = (lo0, lo1)

    barrier = pltpu.get_barrier_semaphore()
    for dev in (partner, neighbour, fwd_dev, fwd_src):
        pl.semaphore_signal(barrier, inc=1, device_id=dev, device_id_type=MESH)
    pl.semaphore_wait(barrier, 4)

    def copy_to(slot, h, k, start, count, dst_start, dev=None, rsem=None):
        if dev is None:
            dev = partner if k == 0 else neighbour
        if rsem is None:
            rsem = recv_sem.at[slot, h, k]
        return pltpu.make_async_remote_copy(
            src_ref=wins[slot].at[h, pl.ds(start, count)],
            dst_ref=wins[slot].at[h, pl.ds(dst_start, count)],
            send_sem=send_sem.at[slot, h, k], recv_sem=rsem,
            device_id=dev, device_id_type=MESH)

    def part_block(slot, jj, incoming=False):
        if incoming:
            return copy_to(slot, 1, 0, part_pos + jj, 1, part_pos + jj, rsem=part_sem.at[slot, jj])
        return copy_to(slot, 1, 0, own_pos + jj, 1, own_pos + jj, rsem=part_sem.at[slot, jj])

    def forward(slot, jj):
        part_block(slot, jj, incoming=True).wait_recv()
        copy_to(slot, 1, 1, part_pos + jj, 1, halo_pos + jj, dev=fwd_dev).start()

    kh = win0.shape[2]

    def load_targets(b, carry):
        tf = jnp.transpose(tgt_in[b].astype(jnp.float32))
        for h in range(HALVES):
            part = tf[h * kh:(h + 1) * kh]
            tgt_ref[h, b] = part
            win0[h, half + b] = part
        return carry

    lax.fori_loop(0, 2 * half, load_targets, 0)
    for h in range(HALVES):
        copy_to(0, h, 1, own_pos, half, nb_halo_pos).start()

    own_copy = pltpu.make_async_copy(trans_hbm.at[:, pl.ds(half * c, half)], t_own, tsem.at[0])
    own_copy.start()
    oth_copy = pltpu.make_async_remote_copy(
        src_ref=trans_hbm.at[:, pl.ds(half * (1 - c), half)], dst_ref=t_oth,
        send_sem=tsem.at[1], recv_sem=tsem.at[2], device_id=partner, device_id_type=MESH)
    oth_copy.start()
    for h in range(HALVES):
        split_blocks(win0, hi0, lo0, h, half, 2 * half)

    def prep(tv, first):
        def body(k, carry):
            al = k // half
            jj = k % half
            for t in range(tv.shape[2]):
                v = jnp.transpose(tv[al, jj, t])
                b = v.astype(jnp.bfloat16)
                thi[first + al, jj, pl.ds(t * tile, tile), :] = b
                tlo[first + al, jj, pl.ds(t * tile, tile), :] = (
                    v - b.astype(jnp.float32)).astype(jnp.bfloat16)
            return carry

        lax.fori_loop(0, acts * half, body, 0)

    own_copy.wait()
    prep(t_own, 0)
    oth_copy.wait_send()
    oth_copy.wait_recv()
    prep(t_oth, acts)

    def stage(h, src, dst, first=False, halo=True):
        if first:
            done = copy_to(src, h, 1, own_pos, half, halo_pos)
            done.wait_send()
            done.wait_recv()
            split_blocks(wins[src], his[src], los[src], h, halo_pos, half)
        elif h == 0:
            for k, start in ((0, part_pos), (1, halo_pos)):
                done = copy_to(src, h, k, own_pos, half, start)
                done.wait_send()
                done.wait_recv()
                split_blocks(wins[src], his[src], los[src], h, start, half)
        else:
            copy_to(src, h, 0, own_pos, half, part_pos).wait_send()
            split_blocks(wins[src], his[src], los[src], h, part_pos, half)
            done = copy_to(src, h, 1, part_pos, half, halo_pos, dev=fwd_dev)
            done.wait_send()
            done.wait_recv()
            split_blocks(wins[src], his[src], los[src], h, halo_pos, half)
        src_hi, src_lo = his[src], los[src]
        dst_win, dst_hi, dst_lo = wins[dst], his[dst], los[dst]

        def block(jj, carry):
            j = half * c + jj
            best = None
            for ab in range(2 * acts):
                a = lax.rem(2 * c + ab, 2 * acts)
                p0 = pos_ref[a, j, 0]
                p1 = pos_ref[a, j, 1]
                vh = jnp.concatenate([src_hi[h, p0], src_hi[h, p1]], axis=1)
                vl = jnp.concatenate([src_lo[h, p0], src_lo[h, p1]], axis=1)
                th = thi[ab, jj]
                tl = tlo[ab, jj]
                q = jnp.dot(vh, th, preferred_element_type=jnp.float32)
                q = q + jnp.dot(vl, th, preferred_element_type=jnp.float32)
                q = q + jnp.dot(vh, tl, preferred_element_type=jnp.float32)
                best = q if best is None else jnp.maximum(best, q)
            val = jnp.where(tgt_ref[h, j] == 1.0, jnp.float32(1.0), best)
            dst_win[h, own_pos + jj] = val
            b = val.astype(jnp.bfloat16)
            dst_hi[h, own_pos + jj] = b
            dst_lo[h, own_pos + jj] = (val - b.astype(jnp.float32)).astype(jnp.bfloat16)
            if h == 0:
                copy_to(dst, h, 0, own_pos + jj, 1, own_pos + jj).start()
                if halo:
                    copy_to(dst, h, 1, own_pos + jj, 1, nb_halo_pos + jj).start()
            else:
                part_block(dst, jj).start()
            return carry

        def block_fwd(jj, carry):
            block(jj, carry)
            forward(dst, jj - LAG)
            return carry

        if h == 1 and halo:
            lax.fori_loop(0, LAG, block, 0)
            lax.fori_loop(LAG, half, block_fwd, 0)
        else:
            lax.fori_loop(0, half, block, 0)
        if h == 1 and halo:
            for jj in range(half - LAG, half):
                forward(dst, jj)

    for h in range(HALVES):
        stage(h, 0, 1, first=True)

    def pair(k, carry):
        for h in range(HALVES):
            stage(h, 1, 0)
        for h in range(HALVES):
            stage(h, 0, 1)
        return carry

    lax.fori_loop(0, SWEEPS // 2 - 1, pair, 0)
    for h in range(HALVES):
        stage(h, 1, 0, halo=False)
    done = copy_to(0, 0, 0, own_pos, half, part_pos)
    done.wait_send()
    done.wait_recv()
    copy_to(0, 1, 0, own_pos, half, part_pos).wait_send()
    for jj in range(half):
        part_block(0, jj, incoming=True).wait_recv()

    def store_out(b, carry):
        both = jnp.concatenate([win0[h, half + b] for h in range(HALVES)], axis=0)
        out_ref[b] = jnp.transpose(both)
        return carry

    lax.fori_loop(0, 2 * half, store_out, 0)


def per_device(transitions, columns, targets):
    n_states = lax.axis_size("states")
    rb = transitions.shape[1]
    tile = transitions.shape[3]
    ksets = targets.shape[1]
    kh = ksets // HALVES
    total_blocks = rb * n_states
    first = lax.axis_index("states") * rb - REACH
    pos = lax.rem(columns - first + 2 * total_blocks, total_blocks).astype(jnp.int32)
    tgt = targets.reshape(rb, tile, ksets)
    half = rb // 2
    wshape = (HALVES, rb + 2 * REACH, kh, tile)
    out = pl.pallas_call(
        functools.partial(sweep_kernel, n_states),
        out_shape=jax.ShapeDtypeStruct((rb, tile, ksets), jnp.float32),
        in_specs=[
            pl.BlockSpec(memory_space=pltpu.SMEM),
            pl.BlockSpec(memory_space=pl.ANY),
            pl.BlockSpec(memory_space=pltpu.VMEM),
        ],
        out_specs=pl.BlockSpec(memory_space=pltpu.VMEM),
        scratch_shapes=[
            pltpu.VMEM(wshape, jnp.float32),
            pltpu.VMEM(wshape, jnp.float32),
            pltpu.VMEM(wshape, jnp.bfloat16),
            pltpu.VMEM(wshape, jnp.bfloat16),
            pltpu.VMEM(wshape, jnp.bfloat16),
            pltpu.VMEM(wshape, jnp.bfloat16),
            pltpu.VMEM((transitions.shape[0], half) + transitions.shape[2:], jnp.float32),
            pltpu.VMEM((transitions.shape[0], half) + transitions.shape[2:], jnp.float32),
            pltpu.VMEM((2 * transitions.shape[0], half, 2 * tile, tile), jnp.bfloat16),
            pltpu.VMEM((2 * transitions.shape[0], half, 2 * tile, tile), jnp.bfloat16),
            pltpu.VMEM((HALVES, rb, kh, tile), jnp.float32),
            pltpu.SemaphoreType.DMA((3,)),
            pltpu.SemaphoreType.DMA((2, HALVES, 2)),
            pltpu.SemaphoreType.DMA((2, HALVES, 2)),
            pltpu.SemaphoreType.DMA((2, half)),
        ],
        compiler_params=pltpu.CompilerParams(
            collective_id=0, has_side_effects=True, vmem_limit_bytes=60 * 1024 * 1024),
    )(pos, transitions, tgt)
    return out.reshape(rb * tile, ksets)


def solution(mesh):
    return jax.shard_map(
        per_device,
        mesh=mesh,
        in_specs=(P("act", "states", None, None, None), P(None, "states", None), P("states", None)),
        out_specs=P("states", None),
        check_vma=False,
    )
```

```python
import functools

import jax
import jax.numpy as jnp
from jax import lax
from jax.experimental import pallas as pl
from jax.experimental.pallas import tpu as pltpu
from jax.sharding import PartitionSpec as P

REACH = 8
SWEEPS = 12
HALVES = 2
MESH = pl.DeviceIdType.MESH


def split_blocks(src, hi, lo, h, first, count):
    def body(k, carry):
        v = src[h, first + k]
        b = v.astype(jnp.bfloat16)
        hi[h, first + k] = b
        lo[h, first + k] = (v - b.astype(jnp.float32)).astype(jnp.bfloat16)
        return carry

    lax.fori_loop(0, count, body, 0)


def sweep_kernel(n_states, pos_ref, trans_hbm, tgt_in, out_ref,
                 win0, win1, hi0, hi1, lo0, lo1, t_own, t_oth, thi, tlo, tgt_ref,
                 tsem, send_sem, recv_sem):
    i = lax.axis_index("states")
    c = lax.axis_index("act")
    acts = t_own.shape[0]
    half = t_own.shape[1]
    tile = t_own.shape[3]
    own_pos = half + half * c
    part_pos = 2 * half - half * c
    halo_pos = 3 * half * c
    nb_halo_pos = 3 * half * (1 - c)
    partner = (i, 1 - c)
    neighbour = (lax.rem(i + 2 * c - 1 + n_states, n_states), 1 - c)
    wins = (win0, win1)
    his = (hi0, hi1)
    los = (lo0, lo1)

    barrier = pltpu.get_barrier_semaphore()
    for dev in (partner, neighbour):
        pl.semaphore_signal(barrier, inc=1, device_id=dev, device_id_type=MESH)
    pl.semaphore_wait(barrier, 2)

    def copy_to(slot, h, k, start, count, dst_start):
        dev = partner if k == 0 else neighbour
        return pltpu.make_async_remote_copy(
            src_ref=wins[slot].at[h, pl.ds(start, count)],
            dst_ref=wins[slot].at[h, pl.ds(dst_start, count)],
            send_sem=send_sem.at[slot, h, k], recv_sem=recv_sem.at[slot, h, k],
            device_id=dev, device_id_type=MESH)

    kh = win0.shape[2]

    def load_targets(b, carry):
        tf = jnp.transpose(tgt_in[b].astype(jnp.float32))
        for h in range(HALVES):
            part = tf[h * kh:(h + 1) * kh]
            tgt_ref[h, b] = part
            win0[h, half + b] = part
        return carry

    own_copy = pltpu.make_async_copy(trans_hbm.at[:, pl.ds(half * c, half)], t_own, tsem.at[0])
    own_copy.start()
    oth_copy = pltpu.make_async_remote_copy(
        src_ref=trans_hbm.at[:, pl.ds(half * (1 - c), half)], dst_ref=t_oth,
        send_sem=tsem.at[1], recv_sem=tsem.at[2], device_id=partner, device_id_type=MESH)
    oth_copy.start()

    lax.fori_loop(half * c, half * c + half, load_targets, 0)
    for h in range(HALVES):
        copy_to(0, h, 1, own_pos, half, nb_halo_pos).start()
    lax.fori_loop(half * (1 - c), half * (1 - c) + half, load_targets, 0)
    for h in range(HALVES):
        split_blocks(win0, hi0, lo0, h, half, 2 * half)

    def prep(tv, first):
        def body(k, carry):
            al = k // half
            jj = k % half
            for t in range(tv.shape[2]):
                v = jnp.transpose(tv[al, jj, t])
                b = v.astype(jnp.bfloat16)
                thi[first + al, jj, pl.ds(t * tile, tile), :] = b
                tlo[first + al, jj, pl.ds(t * tile, tile), :] = (
                    v - b.astype(jnp.float32)).astype(jnp.bfloat16)
            return carry

        lax.fori_loop(0, acts * half, body, 0)

    own_copy.wait()
    prep(t_own, 0)
    oth_copy.wait_send()
    oth_copy.wait_recv()
    prep(t_oth, acts)

    def stage(h, src, dst, first=False, halo=True):
        if first:
            done = copy_to(src, h, 1, own_pos, half, halo_pos)
            done.wait_send()
            done.wait_recv()
            split_blocks(wins[src], his[src], los[src], h, halo_pos, half)
        else:
            for k, start in ((0, part_pos), (1, halo_pos)):
                done = copy_to(src, h, k, own_pos, half, start)
                done.wait_send()
                done.wait_recv()
                split_blocks(wins[src], his[src], los[src], h, start, half)
        src_hi, src_lo = his[src], los[src]
        dst_win, dst_hi, dst_lo = wins[dst], his[dst], los[dst]

        def block(jj, carry):
            j = half * c + jj
            best = None
            for ab in range(2 * acts):
                a = lax.rem(2 * c + ab, 2 * acts)
                p0 = pos_ref[a, j, 0]
                p1 = pos_ref[a, j, 1]
                vh = jnp.concatenate([src_hi[h, p0], src_hi[h, p1]], axis=1)
                vl = jnp.concatenate([src_lo[h, p0], src_lo[h, p1]], axis=1)
                th = thi[ab, jj]
                tl = tlo[ab, jj]
                q = jnp.dot(vh, th, preferred_element_type=jnp.float32)
                q = q + jnp.dot(vl, th, preferred_element_type=jnp.float32)
                q = q + jnp.dot(vh, tl, preferred_element_type=jnp.float32)
                best = q if best is None else jnp.maximum(best, q)
            val = jnp.where(tgt_ref[h, j] == 1.0, jnp.float32(1.0), best)
            dst_win[h, own_pos + jj] = val
            b = val.astype(jnp.bfloat16)
            dst_hi[h, own_pos + jj] = b
            dst_lo[h, own_pos + jj] = (val - b.astype(jnp.float32)).astype(jnp.bfloat16)
            copy_to(dst, h, 0, own_pos + jj, 1, own_pos + jj).start()
            if halo:
                copy_to(dst, h, 1, own_pos + jj, 1, nb_halo_pos + jj).start()
            return carry

        lax.fori_loop(0, half, block, 0)

    for h in range(HALVES):
        stage(h, 0, 1, first=True)

    def pair(k, carry):
        for h in range(HALVES):
            stage(h, 1, 0)
        for h in range(HALVES):
            stage(h, 0, 1)
        return carry

    lax.fori_loop(0, SWEEPS // 2 - 1, pair, 0)
    for h in range(HALVES):
        stage(h, 1, 0, halo=False)
    for h in range(HALVES):
        done = copy_to(0, h, 0, own_pos, half, part_pos)
        done.wait_send()
        done.wait_recv()

    def store_out(b, carry):
        both = jnp.concatenate([win0[h, half + b] for h in range(HALVES)], axis=0)
        out_ref[b] = jnp.transpose(both)
        return carry

    lax.fori_loop(0, 2 * half, store_out, 0)


def per_device(transitions, columns, targets):
    n_states = lax.axis_size("states")
    rb = transitions.shape[1]
    tile = transitions.shape[3]
    ksets = targets.shape[1]
    kh = ksets // HALVES
    total_blocks = rb * n_states
    first = lax.axis_index("states") * rb - REACH
    pos = lax.rem(columns - first + 2 * total_blocks, total_blocks).astype(jnp.int32)
    tgt = targets.reshape(rb, tile, ksets)
    half = rb // 2
    wshape = (HALVES, rb + 2 * REACH, kh, tile)
    out = pl.pallas_call(
        functools.partial(sweep_kernel, n_states),
        out_shape=jax.ShapeDtypeStruct((rb, tile, ksets), jnp.float32),
        in_specs=[
            pl.BlockSpec(memory_space=pltpu.SMEM),
            pl.BlockSpec(memory_space=pl.ANY),
            pl.BlockSpec(memory_space=pltpu.VMEM),
        ],
        out_specs=pl.BlockSpec(memory_space=pltpu.VMEM),
        scratch_shapes=[
            pltpu.VMEM(wshape, jnp.float32),
            pltpu.VMEM(wshape, jnp.float32),
            pltpu.VMEM(wshape, jnp.bfloat16),
            pltpu.VMEM(wshape, jnp.bfloat16),
            pltpu.VMEM(wshape, jnp.bfloat16),
            pltpu.VMEM(wshape, jnp.bfloat16),
            pltpu.VMEM((transitions.shape[0], half) + transitions.shape[2:], jnp.float32),
            pltpu.VMEM((transitions.shape[0], half) + transitions.shape[2:], jnp.float32),
            pltpu.VMEM((2 * transitions.shape[0], half, 2 * tile, tile), jnp.bfloat16),
            pltpu.VMEM((2 * transitions.shape[0], half, 2 * tile, tile), jnp.bfloat16),
            pltpu.VMEM((HALVES, rb, kh, tile), jnp.float32),
            pltpu.SemaphoreType.DMA((3,)),
            pltpu.SemaphoreType.DMA((2, HALVES, 2)),
            pltpu.SemaphoreType.DMA((2, HALVES, 2)),
        ],
        compiler_params=pltpu.CompilerParams(
            collective_id=0, has_side_effects=True, vmem_limit_bytes=60 * 1024 * 1024),
    )(pos, transitions, tgt)
    return out.reshape(rb * tile, ksets)


def solution(mesh):
    return jax.shard_map(
        per_device,
        mesh=mesh,
        in_specs=(P("act", "states", None, None, None), P(None, "states", None), P("states", None)),
        out_specs=P("states", None),
        check_vma=False,
    )
```

```python
import functools

import jax
import jax.numpy as jnp
from jax import lax
from jax.experimental import pallas as pl
from jax.experimental.pallas import tpu as pltpu
from jax.sharding import PartitionSpec as P

REACH = 8
SWEEPS = 12
HALVES = 2
MESH = pl.DeviceIdType.MESH


def split_blocks(src, hi, lo, h, first, count):
    def body(k, carry):
        v = src[h, first + k]
        b = v.astype(jnp.bfloat16)
        hi[h, first + k] = b
        lo[h, first + k] = (v - b.astype(jnp.float32)).astype(jnp.bfloat16)
        return carry

    lax.fori_loop(0, count, body, 0)


def sweep_kernel(n_states, pos_ref, trans_hbm, tgt_in, out_ref,
                 win0, win1, hi0, hi1, lo0, lo1, t_own, t_oth, thi, tlo, tgt_ref,
                 tsem, send_sem, recv_sem):
    i = lax.axis_index("states")
    c = lax.axis_index("act")
    acts = t_own.shape[0]
    half = t_own.shape[1]
    tile = t_own.shape[3]
    own_pos = half + half * c
    part_pos = 2 * half - half * c
    halo_pos = 3 * half * c
    nb_halo_pos = 3 * half * (1 - c)
    partner = (i, 1 - c)
    neighbour = (lax.rem(i + 2 * c - 1 + n_states, n_states), 1 - c)
    wins = (win0, win1)
    his = (hi0, hi1)
    los = (lo0, lo1)

    barrier = pltpu.get_barrier_semaphore()
    for dev in (partner, neighbour):
        pl.semaphore_signal(barrier, inc=1, device_id=dev, device_id_type=MESH)
    pl.semaphore_wait(barrier, 2)

    def copy_to(slot, h, k, start, count, dst_start):
        dev = partner if k == 0 else neighbour
        return pltpu.make_async_remote_copy(
            src_ref=wins[slot].at[h, pl.ds(start, count)],
            dst_ref=wins[slot].at[h, pl.ds(dst_start, count)],
            send_sem=send_sem.at[slot, h, k], recv_sem=recv_sem.at[slot, h, k],
            device_id=dev, device_id_type=MESH)

    kh = win0.shape[2]

    def load_targets(b, carry):
        tf = jnp.transpose(tgt_in[b].astype(jnp.float32))
        for h in range(HALVES):
            part = tf[h * kh:(h + 1) * kh]
            tgt_ref[h, b] = part
            win0[h, half + b] = part
        return carry

    own_copy = pltpu.make_async_copy(trans_hbm.at[:, pl.ds(half * c, half)], t_own, tsem.at[0])
    own_copy.start()
    oth_copy = pltpu.make_async_remote_copy(
        src_ref=trans_hbm.at[:, pl.ds(half * (1 - c), half)], dst_ref=t_oth,
        send_sem=tsem.at[1], recv_sem=tsem.at[2], device_id=partner, device_id_type=MESH)
    oth_copy.start()

    lax.fori_loop(half * c, half * c + half, load_targets, 0)
    for h in range(HALVES):
        copy_to(0, h, 1, own_pos, half, nb_halo_pos).start()
    lax.fori_loop(half * (1 - c), half * (1 - c) + half, load_targets, 0)
    for h in range(HALVES):
        split_blocks(win0, hi0, lo0, h, half, 2 * half)

    def prep(tv, first):
        def body(k, carry):
            al = k // half
            jj = k % half
            for t in range(tv.shape[2]):
                v = jnp.transpose(tv[al, jj, t])
                b = v.astype(jnp.bfloat16)
                thi[first + al, jj, pl.ds(t * tile, tile), :] = b
                tlo[first + al, jj, pl.ds(t * tile, tile), :] = (
                    v - b.astype(jnp.float32)).astype(jnp.bfloat16)
            return carry

        lax.fori_loop(0, acts * half, body, 0)

    own_copy.wait()
    prep(t_own, 0)
    oth_copy.wait_send()
    oth_copy.wait_recv()
    prep(t_oth, acts)

    def stage(h, src, dst, first=False, halo=True):
        if first:
            done = copy_to(src, h, 1, own_pos, half, halo_pos)
            done.wait_send()
            done.wait_recv()
            split_blocks(wins[src], his[src], los[src], h, halo_pos, half)
        else:
            for k, start in ((0, part_pos), (1, halo_pos)):
                done = copy_to(src, h, k, own_pos, half, start)
                done.wait_send()
                done.wait_recv()
                split_blocks(wins[src], his[src], los[src], h, start, half)
        src_hi, src_lo = his[src], los[src]
        dst_win, dst_hi, dst_lo = wins[dst], his[dst], los[dst]

        def block(jj, carry):
            j = half * c + jj
            best = None
            for ab in range(2 * acts):
                a = lax.rem(2 * c + ab, 2 * acts)
                p0 = pos_ref[a, j, 0]
                p1 = pos_ref[a, j, 1]
                vh = jnp.concatenate([src_hi[h, p0], src_hi[h, p1]], axis=1)
                vl = jnp.concatenate([src_lo[h, p0], src_lo[h, p1]], axis=1)
                th = thi[ab, jj]
                tl = tlo[ab, jj]
                q = jnp.dot(vh, th, preferred_element_type=jnp.float32)
                q = q + jnp.dot(vl, th, preferred_element_type=jnp.float32)
                q = q + jnp.dot(vh, tl, preferred_element_type=jnp.float32)
                best = q if best is None else jnp.maximum(best, q)
            val = jnp.where(tgt_ref[h, j] == 1.0, jnp.float32(1.0), best)
            dst_win[h, own_pos + jj] = val
            b = val.astype(jnp.bfloat16)
            dst_hi[h, own_pos + jj] = b
            dst_lo[h, own_pos + jj] = (val - b.astype(jnp.float32)).astype(jnp.bfloat16)
            if halo:
                copy_to(dst, h, 1, own_pos + jj, 1, nb_halo_pos + jj).start()
            copy_to(dst, h, 0, own_pos + jj, 1, own_pos + jj).start()
            return carry

        lax.fori_loop(0, half, block, 0)

    for h in range(HALVES):
        stage(h, 0, 1, first=True)

    def pair(k, carry):
        for h in range(HALVES):
            stage(h, 1, 0)
        for h in range(HALVES):
            stage(h, 0, 1)
        return carry

    lax.fori_loop(0, SWEEPS // 2 - 1, pair, 0)
    for h in range(HALVES):
        stage(h, 1, 0, halo=False)
    for h in range(HALVES):
        done = copy_to(0, h, 0, own_pos, half, part_pos)
        done.wait_send()
        done.wait_recv()

    def store_out(b, carry):
        both = jnp.concatenate([win0[h, half + b] for h in range(HALVES)], axis=0)
        out_ref[b] = jnp.transpose(both)
        return carry

    lax.fori_loop(0, 2 * half, store_out, 0)


def per_device(transitions, columns, targets):
    n_states = lax.axis_size("states")
    rb = transitions.shape[1]
    tile = transitions.shape[3]
    ksets = targets.shape[1]
    kh = ksets // HALVES
    total_blocks = rb * n_states
    first = lax.axis_index("states") * rb - REACH
    pos = lax.rem(columns - first + 2 * total_blocks, total_blocks).astype(jnp.int32)
    tgt = targets.reshape(rb, tile, ksets)
    half = rb // 2
    wshape = (HALVES, rb + 2 * REACH, kh, tile)
    out = pl.pallas_call(
        functools.partial(sweep_kernel, n_states),
        out_shape=jax.ShapeDtypeStruct((rb, tile, ksets), jnp.float32),
        in_specs=[
            pl.BlockSpec(memory_space=pltpu.SMEM),
            pl.BlockSpec(memory_space=pl.ANY),
            pl.BlockSpec(memory_space=pltpu.VMEM),
        ],
        out_specs=pl.BlockSpec(memory_space=pltpu.VMEM),
        scratch_shapes=[
            pltpu.VMEM(wshape, jnp.float32),
            pltpu.VMEM(wshape, jnp.float32),
            pltpu.VMEM(wshape, jnp.bfloat16),
            pltpu.VMEM(wshape, jnp.bfloat16),
            pltpu.VMEM(wshape, jnp.bfloat16),
            pltpu.VMEM(wshape, jnp.bfloat16),
            pltpu.VMEM((transitions.shape[0], half) + transitions.shape[2:], jnp.float32),
            pltpu.VMEM((transitions.shape[0], half) + transitions.shape[2:], jnp.float32),
            pltpu.VMEM((2 * transitions.shape[0], half, 2 * tile, tile), jnp.bfloat16),
            pltpu.VMEM((2 * transitions.shape[0], half, 2 * tile, tile), jnp.bfloat16),
            pltpu.VMEM((HALVES, rb, kh, tile), jnp.float32),
            pltpu.SemaphoreType.DMA((3,)),
            pltpu.SemaphoreType.DMA((2, HALVES, 2)),
            pltpu.SemaphoreType.DMA((2, HALVES, 2)),
        ],
        compiler_params=pltpu.CompilerParams(
            collective_id=0, has_side_effects=True, vmem_limit_bytes=60 * 1024 * 1024),
    )(pos, transitions, tgt)
    return out.reshape(rb * tile, ksets)


def solution(mesh):
    return jax.shard_map(
        per_device,
        mesh=mesh,
        in_specs=(P("act", "states", None, None, None), P(None, "states", None), P("states", None)),
        out_specs=P("states", None),
        check_vma=False,
    )
```

```python
import functools

import jax
import jax.numpy as jnp
from jax import lax
from jax.experimental import pallas as pl
from jax.experimental.pallas import tpu as pltpu
from jax.sharding import PartitionSpec as P

REACH = 8
SWEEPS = 12
HALVES = 2
MESH = pl.DeviceIdType.MESH


def split_blocks(src, hi, lo, h, first, count):
    def body(k, carry):
        v = src[h, first + k]
        b = v.astype(jnp.bfloat16)
        hi[h, first + k] = b
        lo[h, first + k] = (v - b.astype(jnp.float32)).astype(jnp.bfloat16)
        return carry

    lax.fori_loop(0, count, body, 0)


def sweep_kernel(n_states, pos_ref, trans_hbm, tgt_in, out_ref,
                 win0, win1, hi0, hi1, lo0, lo1, t_own, t_oth, thi, tlo, tgt_ref,
                 tsem, send_sem, recv_sem):
    i = lax.axis_index("states")
    c = lax.axis_index("act")
    acts = t_own.shape[0]
    half = t_own.shape[1]
    tile = t_own.shape[3]
    own_pos = half + half * c
    part_pos = 2 * half - half * c
    halo_pos = 3 * half * c
    nb_halo_pos = 3 * half * (1 - c)
    partner = (i, 1 - c)
    neighbour = (lax.rem(i + 2 * c - 1 + n_states, n_states), 1 - c)
    wins = (win0, win1)
    his = (hi0, hi1)
    los = (lo0, lo1)

    barrier = pltpu.get_barrier_semaphore()
    for dev in (partner, neighbour):
        pl.semaphore_signal(barrier, inc=1, device_id=dev, device_id_type=MESH)
    pl.semaphore_wait(barrier, 2)

    def copy_to(slot, h, k, start, count, dst_start):
        dev = partner if k == 0 else neighbour
        return pltpu.make_async_remote_copy(
            src_ref=wins[slot].at[h, pl.ds(start, count)],
            dst_ref=wins[slot].at[h, pl.ds(dst_start, count)],
            send_sem=send_sem.at[slot, h, k], recv_sem=recv_sem.at[slot, h, k],
            device_id=dev, device_id_type=MESH)

    kh = win0.shape[2]

    def load_targets(b, carry):
        tf = jnp.transpose(tgt_in[b].astype(jnp.float32))
        for h in range(HALVES):
            part = tf[h * kh:(h + 1) * kh]
            tgt_ref[h, b] = part
            win0[h, half + b] = part
        return carry

    own_copy = pltpu.make_async_copy(trans_hbm.at[:, pl.ds(half * c, half)], t_own, tsem.at[0])
    own_copy.start()
    oth_copy = pltpu.make_async_remote_copy(
        src_ref=trans_hbm.at[:, pl.ds(half * (1 - c), half)], dst_ref=t_oth,
        send_sem=tsem.at[1], recv_sem=tsem.at[2], device_id=partner, device_id_type=MESH)
    oth_copy.start()

    lax.fori_loop(half * c, half * c + half, load_targets, 0)
    for h in range(HALVES):
        copy_to(0, h, 1, own_pos, half, nb_halo_pos).start()
    lax.fori_loop(half * (1 - c), half * (1 - c) + half, load_targets, 0)
    for h in range(HALVES):
        split_blocks(win0, hi0, lo0, h, half, 2 * half)

    def prep(tv, first):
        def body(k, carry):
            al = k // half
            jj = k % half
            for t in range(tv.shape[2]):
                v = jnp.transpose(tv[al, jj, t])
                b = v.astype(jnp.bfloat16)
                thi[first + al, jj, pl.ds(t * tile, tile), :] = b
                tlo[first + al, jj, pl.ds(t * tile, tile), :] = (
                    v - b.astype(jnp.float32)).astype(jnp.bfloat16)
            return carry

        lax.fori_loop(0, acts * half, body, 0)

    own_copy.wait()
    prep(t_own, 0)
    oth_copy.wait_send()
    oth_copy.wait_recv()
    prep(t_oth, acts)

    def stage(h, src, dst, first=False, halo=True):
        if first:
            done = copy_to(src, h, 1, own_pos, half, halo_pos)
            done.wait_send()
            done.wait_recv()
            split_blocks(wins[src], his[src], los[src], h, halo_pos, half)
        else:
            for k, start in ((0, part_pos), (1, halo_pos)):
                done = copy_to(src, h, k, own_pos, half, start)
                done.wait_send()
                done.wait_recv()
                split_blocks(wins[src], his[src], los[src], h, start, half)
        src_hi, src_lo = his[src], los[src]
        dst_win, dst_hi, dst_lo = wins[dst], his[dst], los[dst]

        def block(jj, carry):
            j = half * c + jj
            best = None
            for ab in range(2 * acts):
                a = lax.rem(2 * c + ab, 2 * acts)
                p0 = pos_ref[a, j, 0]
                p1 = pos_ref[a, j, 1]
                vh = jnp.concatenate([src_hi[h, p0], src_hi[h, p1]], axis=1)
                vl = jnp.concatenate([src_lo[h, p0], src_lo[h, p1]], axis=1)
                th = thi[ab, jj]
                tl = tlo[ab, jj]
                q = jnp.dot(vh, th, preferred_element_type=jnp.float32)
                q = q + jnp.dot(vl, th, preferred_element_type=jnp.float32)
                q = q + jnp.dot(vh, tl, preferred_element_type=jnp.float32)
                best = q if best is None else jnp.maximum(best, q)
            val = jnp.where(tgt_ref[h, j] == 1.0, jnp.float32(1.0), best)
            dst_win[h, own_pos + jj] = val
            b = val.astype(jnp.bfloat16)
            dst_hi[h, own_pos + jj] = b
            dst_lo[h, own_pos + jj] = (val - b.astype(jnp.float32)).astype(jnp.bfloat16)
            if halo:
                copy_to(dst, h, 1, own_pos + jj, 1, nb_halo_pos + jj).start()
            copy_to(dst, h, 0, own_pos + jj, 1, own_pos + jj).start()
            return carry

        lax.fori_loop(0, half, block, 0)

    for h in range(HALVES):
        stage(h, 0, 1, first=True)

    def pair(k, carry):
        for h in range(HALVES):
            stage(h, 1, 0)
        for h in range(HALVES):
            stage(h, 0, 1)
        return carry

    lax.fori_loop(0, SWEEPS // 2 - 1, pair, 0)
    for h in range(HALVES):
        stage(h, 1, 0, halo=False)

    def store_out(b, carry):
        both = jnp.concatenate([win0[h, half + b] for h in range(HALVES)], axis=0)
        out_ref[b] = jnp.transpose(both)
        return carry

    lax.fori_loop(half * c, half * c + half, store_out, 0)
    for h in range(HALVES):
        done = copy_to(0, h, 0, own_pos, half, part_pos)
        done.wait_send()
        done.wait_recv()
    lax.fori_loop(half * (1 - c), half * (1 - c) + half, store_out, 0)


def per_device(transitions, columns, targets):
    n_states = lax.axis_size("states")
    rb = transitions.shape[1]
    tile = transitions.shape[3]
    ksets = targets.shape[1]
    kh = ksets // HALVES
    total_blocks = rb * n_states
    first = lax.axis_index("states") * rb - REACH
    pos = lax.rem(columns - first + 2 * total_blocks, total_blocks).astype(jnp.int32)
    tgt = targets.reshape(rb, tile, ksets)
    half = rb // 2
    wshape = (HALVES, rb + 2 * REACH, kh, tile)
    out = pl.pallas_call(
        functools.partial(sweep_kernel, n_states),
        out_shape=jax.ShapeDtypeStruct((rb, tile, ksets), jnp.float32),
        in_specs=[
            pl.BlockSpec(memory_space=pltpu.SMEM),
            pl.BlockSpec(memory_space=pl.ANY),
            pl.BlockSpec(memory_space=pltpu.VMEM),
        ],
        out_specs=pl.BlockSpec(memory_space=pltpu.VMEM),
        scratch_shapes=[
            pltpu.VMEM(wshape, jnp.float32),
            pltpu.VMEM(wshape, jnp.float32),
            pltpu.VMEM(wshape, jnp.bfloat16),
            pltpu.VMEM(wshape, jnp.bfloat16),
            pltpu.VMEM(wshape, jnp.bfloat16),
            pltpu.VMEM(wshape, jnp.bfloat16),
            pltpu.VMEM((transitions.shape[0], half) + transitions.shape[2:], jnp.float32),
            pltpu.VMEM((transitions.shape[0], half) + transitions.shape[2:], jnp.float32),
            pltpu.VMEM((2 * transitions.shape[0], half, 2 * tile, tile), jnp.bfloat16),
            pltpu.VMEM((2 * transitions.shape[0], half, 2 * tile, tile), jnp.bfloat16),
            pltpu.VMEM((HALVES, rb, kh, tile), jnp.float32),
            pltpu.SemaphoreType.DMA((3,)),
            pltpu.SemaphoreType.DMA((2, HALVES, 2)),
            pltpu.SemaphoreType.DMA((2, HALVES, 2)),
        ],
        compiler_params=pltpu.CompilerParams(
            collective_id=0, has_side_effects=True, vmem_limit_bytes=60 * 1024 * 1024),
    )(pos, transitions, tgt)
    return out.reshape(rb * tile, ksets)


def solution(mesh):
    return jax.shard_map(
        per_device,
        mesh=mesh,
        in_specs=(P("act", "states", None, None, None), P(None, "states", None), P("states", None)),
        out_specs=P("states", None),
        check_vma=False,
    )
```

```python
import functools

import jax
import jax.numpy as jnp
from jax import lax
from jax.experimental import pallas as pl
from jax.experimental.pallas import tpu as pltpu
from jax.sharding import PartitionSpec as P

REACH = 8
SWEEPS = 12
HALVES = 4
MESH = pl.DeviceIdType.MESH


def split_blocks(src, hi, lo, h, first, count):
    def body(k, carry):
        v = src[h, first + k]
        b = v.astype(jnp.bfloat16)
        hi[h, first + k] = b
        lo[h, first + k] = (v - b.astype(jnp.float32)).astype(jnp.bfloat16)
        return carry

    lax.fori_loop(0, count, body, 0)


def sweep_kernel(n_states, pos_ref, trans_hbm, tgt_in, out_ref,
                 win0, win1, hi0, hi1, lo0, lo1, t_own, t_oth, thi, tlo, tgt_ref,
                 tsem, send_sem, recv_sem):
    i = lax.axis_index("states")
    c = lax.axis_index("act")
    acts = t_own.shape[0]
    half = t_own.shape[1]
    tile = t_own.shape[3]
    own_pos = half + half * c
    part_pos = 2 * half - half * c
    halo_pos = 3 * half * c
    nb_halo_pos = 3 * half * (1 - c)
    partner = (i, 1 - c)
    neighbour = (lax.rem(i + 2 * c - 1 + n_states, n_states), 1 - c)
    wins = (win0, win1)
    his = (hi0, hi1)
    los = (lo0, lo1)

    barrier = pltpu.get_barrier_semaphore()
    for dev in (partner, neighbour):
        pl.semaphore_signal(barrier, inc=1, device_id=dev, device_id_type=MESH)
    pl.semaphore_wait(barrier, 2)

    def copy_to(slot, h, k, start, count, dst_start):
        dev = partner if k == 0 else neighbour
        return pltpu.make_async_remote_copy(
            src_ref=wins[slot].at[h, pl.ds(start, count)],
            dst_ref=wins[slot].at[h, pl.ds(dst_start, count)],
            send_sem=send_sem.at[slot, h, k], recv_sem=recv_sem.at[slot, h, k],
            device_id=dev, device_id_type=MESH)

    kh = win0.shape[2]

    def load_targets(b, carry):
        tf = jnp.transpose(tgt_in[b].astype(jnp.float32))
        for h in range(HALVES):
            part = tf[h * kh:(h + 1) * kh]
            tgt_ref[h, b] = part
            win0[h, half + b] = part
        return carry

    own_copy = pltpu.make_async_copy(trans_hbm.at[:, pl.ds(half * c, half)], t_own, tsem.at[0])
    own_copy.start()
    oth_copy = pltpu.make_async_remote_copy(
        src_ref=trans_hbm.at[:, pl.ds(half * (1 - c), half)], dst_ref=t_oth,
        send_sem=tsem.at[1], recv_sem=tsem.at[2], device_id=partner, device_id_type=MESH)
    oth_copy.start()

    lax.fori_loop(half * c, half * c + half, load_targets, 0)
    for h in range(HALVES):
        copy_to(0, h, 1, own_pos, half, nb_halo_pos).start()
    lax.fori_loop(half * (1 - c), half * (1 - c) + half, load_targets, 0)
    for h in range(HALVES):
        split_blocks(win0, hi0, lo0, h, half, 2 * half)

    def prep(tv, first):
        def body(k, carry):
            al = k // half
            jj = k % half
            for t in range(tv.shape[2]):
                v = jnp.transpose(tv[al, jj, t])
                b = v.astype(jnp.bfloat16)
                thi[first + al, jj, pl.ds(t * tile, tile), :] = b
                tlo[first + al, jj, pl.ds(t * tile, tile), :] = (
                    v - b.astype(jnp.float32)).astype(jnp.bfloat16)
            return carry

        lax.fori_loop(0, acts * half, body, 0)

    own_copy.wait()
    prep(t_own, 0)
    oth_copy.wait_send()
    oth_copy.wait_recv()
    prep(t_oth, acts)

    def stage(h, src, dst, first=False, halo=True):
        if first:
            done = copy_to(src, h, 1, own_pos, half, halo_pos)
            done.wait_send()
            done.wait_recv()
            split_blocks(wins[src], his[src], los[src], h, halo_pos, half)
        else:
            for k, start in ((0, part_pos), (1, halo_pos)):
                done = copy_to(src, h, k, own_pos, half, start)
                done.wait_send()
                done.wait_recv()
                split_blocks(wins[src], his[src], los[src], h, start, half)
        src_hi, src_lo = his[src], los[src]
        dst_win, dst_hi, dst_lo = wins[dst], his[dst], los[dst]

        def block(jj, carry):
            j = half * c + jj
            best = None
            for ab in range(2 * acts):
                a = lax.rem(2 * c + ab, 2 * acts)
                p0 = pos_ref[a, j, 0]
                p1 = pos_ref[a, j, 1]
                vh = jnp.concatenate([src_hi[h, p0], src_hi[h, p1]], axis=1)
                vl = jnp.concatenate([src_lo[h, p0], src_lo[h, p1]], axis=1)
                th = thi[ab, jj]
                tl = tlo[ab, jj]
                q = jnp.dot(vh, th, preferred_element_type=jnp.float32)
                q = q + jnp.dot(vl, th, preferred_element_type=jnp.float32)
                q = q + jnp.dot(vh, tl, preferred_element_type=jnp.float32)
                best = q if best is None else jnp.maximum(best, q)
            val = jnp.where(tgt_ref[h, j] == 1.0, jnp.float32(1.0), best)
            dst_win[h, own_pos + jj] = val
            b = val.astype(jnp.bfloat16)
            dst_hi[h, own_pos + jj] = b
            dst_lo[h, own_pos + jj] = (val - b.astype(jnp.float32)).astype(jnp.bfloat16)
            if halo:
                copy_to(dst, h, 1, own_pos + jj, 1, nb_halo_pos + jj).start()
            copy_to(dst, h, 0, own_pos + jj, 1, own_pos + jj).start()
            return carry

        lax.fori_loop(0, half, block, 0)

    for h in range(HALVES):
        stage(h, 0, 1, first=True)

    def pair(k, carry):
        for h in range(HALVES):
            stage(h, 1, 0)
        for h in range(HALVES):
            stage(h, 0, 1)
        return carry

    lax.fori_loop(0, SWEEPS // 2 - 1, pair, 0)
    for h in range(HALVES):
        stage(h, 1, 0, halo=False)

    def store_out(b, carry):
        both = jnp.concatenate([win0[h, half + b] for h in range(HALVES)], axis=0)
        out_ref[b] = jnp.transpose(both)
        return carry

    lax.fori_loop(half * c, half * c + half, store_out, 0)
    for h in range(HALVES):
        done = copy_to(0, h, 0, own_pos, half, part_pos)
        done.wait_send()
        done.wait_recv()
    lax.fori_loop(half * (1 - c), half * (1 - c) + half, store_out, 0)


def per_device(transitions, columns, targets):
    n_states = lax.axis_size("states")
    rb = transitions.shape[1]
    tile = transitions.shape[3]
    ksets = targets.shape[1]
    kh = ksets // HALVES
    total_blocks = rb * n_states
    first = lax.axis_index("states") * rb - REACH
    pos = lax.rem(columns - first + 2 * total_blocks, total_blocks).astype(jnp.int32)
    tgt = targets.reshape(rb, tile, ksets)
    half = rb // 2
    wshape = (HALVES, rb + 2 * REACH, kh, tile)
    out = pl.pallas_call(
        functools.partial(sweep_kernel, n_states),
        out_shape=jax.ShapeDtypeStruct((rb, tile, ksets), jnp.float32),
        in_specs=[
            pl.BlockSpec(memory_space=pltpu.SMEM),
            pl.BlockSpec(memory_space=pl.ANY),
            pl.BlockSpec(memory_space=pltpu.VMEM),
        ],
        out_specs=pl.BlockSpec(memory_space=pltpu.VMEM),
        scratch_shapes=[
            pltpu.VMEM(wshape, jnp.float32),
            pltpu.VMEM(wshape, jnp.float32),
            pltpu.VMEM(wshape, jnp.bfloat16),
            pltpu.VMEM(wshape, jnp.bfloat16),
            pltpu.VMEM(wshape, jnp.bfloat16),
            pltpu.VMEM(wshape, jnp.bfloat16),
            pltpu.VMEM((transitions.shape[0], half) + transitions.shape[2:], jnp.float32),
            pltpu.VMEM((transitions.shape[0], half) + transitions.shape[2:], jnp.float32),
            pltpu.VMEM((2 * transitions.shape[0], half, 2 * tile, tile), jnp.bfloat16),
            pltpu.VMEM((2 * transitions.shape[0], half, 2 * tile, tile), jnp.bfloat16),
            pltpu.VMEM((HALVES, rb, kh, tile), jnp.float32),
            pltpu.SemaphoreType.DMA((3,)),
            pltpu.SemaphoreType.DMA((2, HALVES, 2)),
            pltpu.SemaphoreType.DMA((2, HALVES, 2)),
        ],
        compiler_params=pltpu.CompilerParams(
            collective_id=0, has_side_effects=True, vmem_limit_bytes=60 * 1024 * 1024),
    )(pos, transitions, tgt)
    return out.reshape(rb * tile, ksets)


def solution(mesh):
    return jax.shard_map(
        per_device,
        mesh=mesh,
        in_specs=(P("act", "states", None, None, None), P(None, "states", None), P("states", None)),
        out_specs=P("states", None),
        check_vma=False,
    )
```

```python
import functools

import jax
import jax.numpy as jnp
from jax import lax
from jax.experimental import pallas as pl
from jax.experimental.pallas import tpu as pltpu
from jax.sharding import PartitionSpec as P

REACH = 8
SWEEPS = 12
HALVES = 2
MESH = pl.DeviceIdType.MESH


def split_blocks(src, hi, lo, h, first, count):
    def body(k, carry):
        v = src[h, first + k]
        b = v.astype(jnp.bfloat16)
        hi[h, first + k] = b
        lo[h, first + k] = (v - b.astype(jnp.float32)).astype(jnp.bfloat16)
        return carry

    lax.fori_loop(0, count, body, 0)


def sweep_kernel(n_states, pos_ref, trans_hbm, tgt_in, out_ref,
                 win0, win1, hi0, hi1, lo0, lo1, t_own, t_oth, thi, tlo, tgt_ref,
                 tsem, send_sem, recv_sem):
    i = lax.axis_index("states")
    c = lax.axis_index("act")
    acts = t_own.shape[0]
    half = t_own.shape[1]
    tile = t_own.shape[3]
    own_pos = half + half * c
    part_pos = 2 * half - half * c
    halo_pos = 3 * half * c
    nb_halo_pos = 3 * half * (1 - c)
    partner = (i, 1 - c)
    neighbour = (lax.rem(i + 2 * c - 1 + n_states, n_states), 1 - c)
    wins = (win0, win1)
    his = (hi0, hi1)
    los = (lo0, lo1)

    barrier = pltpu.get_barrier_semaphore()
    for dev in (partner, neighbour):
        pl.semaphore_signal(barrier, inc=1, device_id=dev, device_id_type=MESH)
    pl.semaphore_wait(barrier, 2)

    def copy_to(slot, h, k, start, count, dst_start):
        dev = partner if k == 0 else neighbour
        return pltpu.make_async_remote_copy(
            src_ref=wins[slot].at[h, pl.ds(start, count)],
            dst_ref=wins[slot].at[h, pl.ds(dst_start, count)],
            send_sem=send_sem.at[slot, h, k], recv_sem=recv_sem.at[slot, h, k],
            device_id=dev, device_id_type=MESH)

    kh = win0.shape[2]

    def load_targets(b, carry):
        tf = jnp.transpose(tgt_in[b].astype(jnp.float32))
        for h in range(HALVES):
            part = tf[h * kh:(h + 1) * kh]
            tgt_ref[h, b] = part
            win0[h, half + b] = part
        return carry

    own_copy = pltpu.make_async_copy(trans_hbm.at[:, pl.ds(half * c, half)], t_own, tsem.at[0])
    own_copy.start()
    oth_copy = pltpu.make_async_remote_copy(
        src_ref=trans_hbm.at[:, pl.ds(half * (1 - c), half)], dst_ref=t_oth,
        send_sem=tsem.at[1], recv_sem=tsem.at[2], device_id=partner, device_id_type=MESH)
    oth_copy.start()

    lax.fori_loop(half * c, half * c + half, load_targets, 0)
    for h in range(HALVES):
        copy_to(0, h, 1, own_pos, half, nb_halo_pos).start()
    lax.fori_loop(half * (1 - c), half * (1 - c) + half, load_targets, 0)
    for h in range(HALVES):
        split_blocks(win0, hi0, lo0, h, half, 2 * half)

    def prep(tv, first):
        def body(k, carry):
            al = k // half
            jj = k % half
            for t in range(tv.shape[2]):
                v = jnp.transpose(tv[al, jj, t])
                b = v.astype(jnp.bfloat16)
                thi[first + al, jj, pl.ds(t * tile, tile), :] = b
                tlo[first + al, jj, pl.ds(t * tile, tile), :] = (
                    v - b.astype(jnp.float32)).astype(jnp.bfloat16)
            return carry

        lax.fori_loop(0, acts * half, body, 0)

    own_copy.wait()
    prep(t_own, 0)
    oth_copy.wait_send()
    oth_copy.wait_recv()
    prep(t_oth, acts)

    def stage(h, src, dst, first=False, halo=True):
        if first:
            done = copy_to(src, h, 1, own_pos, half, halo_pos)
            done.wait_send()
            done.wait_recv()
            split_blocks(wins[src], his[src], los[src], h, halo_pos, half)
        else:
            for k, start in ((0, part_pos), (1, halo_pos)):
                done = copy_to(src, h, k, own_pos, half, start)
                done.wait_send()
                done.wait_recv()
                split_blocks(wins[src], his[src], los[src], h, start, half)
        src_hi, src_lo = his[src], los[src]
        dst_win, dst_hi, dst_lo = wins[dst], his[dst], los[dst]

        def block(jj, carry):
            j = half * c + jj
            best = None
            for ab in range(2 * acts):
                a = lax.rem(2 * c + ab, 2 * acts)
                p0 = pos_ref[a, j, 0]
                p1 = pos_ref[a, j, 1]
                vh = jnp.concatenate([src_hi[h, p0], src_hi[h, p1]], axis=1)
                vl = jnp.concatenate([src_lo[h, p0], src_lo[h, p1]], axis=1)
                th = thi[ab, jj]
                tl = tlo[ab, jj]
                q = jnp.dot(vh, th, preferred_element_type=jnp.float32)
                q = q + jnp.dot(vl, th, preferred_element_type=jnp.float32)
                q = q + jnp.dot(vh, tl, preferred_element_type=jnp.float32)
                best = q if best is None else jnp.maximum(best, q)
            val = jnp.where(tgt_ref[h, j] == 1.0, jnp.float32(1.0), best)
            dst_win[h, own_pos + jj] = val
            if halo:
                copy_to(dst, h, 1, own_pos + jj, 1, nb_halo_pos + jj).start()
            copy_to(dst, h, 0, own_pos + jj, 1, own_pos + jj).start()
            b = val.astype(jnp.bfloat16)
            dst_hi[h, own_pos + jj] = b
            dst_lo[h, own_pos + jj] = (val - b.astype(jnp.float32)).astype(jnp.bfloat16)
            return carry

        lax.fori_loop(0, half, block, 0)

    for h in range(HALVES):
        stage(h, 0, 1, first=True)

    def pair(k, carry):
        for h in range(HALVES):
            stage(h, 1, 0)
        for h in range(HALVES):
            stage(h, 0, 1)
        return carry

    lax.fori_loop(0, SWEEPS // 2 - 1, pair, 0)
    for h in range(HALVES):
        stage(h, 1, 0, halo=False)

    def store_out(b, carry):
        both = jnp.concatenate([win0[h, half + b] for h in range(HALVES)], axis=0)
        out_ref[b] = jnp.transpose(both)
        return carry

    lax.fori_loop(half * c, half * c + half, store_out, 0)
    for h in range(HALVES):
        done = copy_to(0, h, 0, own_pos, half, part_pos)
        done.wait_send()
        done.wait_recv()
    lax.fori_loop(half * (1 - c), half * (1 - c) + half, store_out, 0)


def per_device(transitions, columns, targets):
    n_states = lax.axis_size("states")
    rb = transitions.shape[1]
    tile = transitions.shape[3]
    ksets = targets.shape[1]
    kh = ksets // HALVES
    total_blocks = rb * n_states
    first = lax.axis_index("states") * rb - REACH
    pos = lax.rem(columns - first + 2 * total_blocks, total_blocks).astype(jnp.int32)
    tgt = targets.reshape(rb, tile, ksets)
    half = rb // 2
    wshape = (HALVES, rb + 2 * REACH, kh, tile)
    out = pl.pallas_call(
        functools.partial(sweep_kernel, n_states),
        out_shape=jax.ShapeDtypeStruct((rb, tile, ksets), jnp.float32),
        in_specs=[
            pl.BlockSpec(memory_space=pltpu.SMEM),
            pl.BlockSpec(memory_space=pl.ANY),
            pl.BlockSpec(memory_space=pltpu.VMEM),
        ],
        out_specs=pl.BlockSpec(memory_space=pltpu.VMEM),
        scratch_shapes=[
            pltpu.VMEM(wshape, jnp.float32),
            pltpu.VMEM(wshape, jnp.float32),
            pltpu.VMEM(wshape, jnp.bfloat16),
            pltpu.VMEM(wshape, jnp.bfloat16),
            pltpu.VMEM(wshape, jnp.bfloat16),
            pltpu.VMEM(wshape, jnp.bfloat16),
            pltpu.VMEM((transitions.shape[0], half) + transitions.shape[2:], jnp.float32),
            pltpu.VMEM((transitions.shape[0], half) + transitions.shape[2:], jnp.float32),
            pltpu.VMEM((2 * transitions.shape[0], half, 2 * tile, tile), jnp.bfloat16),
            pltpu.VMEM((2 * transitions.shape[0], half, 2 * tile, tile), jnp.bfloat16),
            pltpu.VMEM((HALVES, rb, kh, tile), jnp.float32),
            pltpu.SemaphoreType.DMA((3,)),
            pltpu.SemaphoreType.DMA((2, HALVES, 2)),
            pltpu.SemaphoreType.DMA((2, HALVES, 2)),
        ],
        compiler_params=pltpu.CompilerParams(
            collective_id=0, has_side_effects=True, vmem_limit_bytes=60 * 1024 * 1024),
    )(pos, transitions, tgt)
    return out.reshape(rb * tile, ksets)


def solution(mesh):
    return jax.shard_map(
        per_device,
        mesh=mesh,
        in_specs=(P("act", "states", None, None, None), P(None, "states", None), P("states", None)),
        out_specs=P("states", None),
        check_vma=False,
    )
```

```python
import functools

import jax
import jax.numpy as jnp
from jax import lax
from jax.experimental import pallas as pl
from jax.experimental.pallas import tpu as pltpu
from jax.sharding import PartitionSpec as P

REACH = 8
SWEEPS = 12
HALVES = 2
MESH = pl.DeviceIdType.MESH


def split_blocks(src, hi, lo, h, first, count):
    def body(k, carry):
        v = src[h, first + k]
        b = v.astype(jnp.bfloat16)
        hi[h, first + k] = b
        lo[h, first + k] = (v - b.astype(jnp.float32)).astype(jnp.bfloat16)
        return carry

    lax.fori_loop(0, count, body, 0)


def sweep_kernel(n_states, pos_ref, trans_hbm, tgt_in, out_ref,
                 win0, win1, hi0, hi1, lo0, lo1, t_own, t_oth, thi, tlo, tgt_ref,
                 tsem, send_sem, recv_sem):
    i = lax.axis_index("states")
    c = lax.axis_index("act")
    acts = t_own.shape[0]
    half = t_own.shape[1]
    tile = t_own.shape[3]
    own_pos = half + half * c
    part_pos = 2 * half - half * c
    halo_pos = 3 * half * c
    nb_halo_pos = 3 * half * (1 - c)
    partner = (i, 1 - c)
    neighbour = (lax.rem(i + 2 * c - 1 + n_states, n_states), 1 - c)
    wins = (win0, win1)
    his = (hi0, hi1)
    los = (lo0, lo1)

    barrier = pltpu.get_barrier_semaphore()
    for dev in (partner, neighbour):
        pl.semaphore_signal(barrier, inc=1, device_id=dev, device_id_type=MESH)
    pl.semaphore_wait(barrier, 2)

    def copy_to(slot, h, k, start, count, dst_start):
        dev = partner if k == 0 else neighbour
        return pltpu.make_async_remote_copy(
            src_ref=wins[slot].at[h, pl.ds(start, count)],
            dst_ref=wins[slot].at[h, pl.ds(dst_start, count)],
            send_sem=send_sem.at[slot, h, k], recv_sem=recv_sem.at[slot, h, k],
            device_id=dev, device_id_type=MESH)

    kh = win0.shape[2]

    def load_targets(b, carry):
        tf = jnp.transpose(tgt_in[b].astype(jnp.float32))
        for h in range(HALVES):
            part = tf[h * kh:(h + 1) * kh]
            tgt_ref[h, b] = part
            win0[h, half + b] = part
        return carry

    own_copy = pltpu.make_async_copy(trans_hbm.at[:, pl.ds(half * c, half)], t_own, tsem.at[0])
    own_copy.start()
    oth_copy = pltpu.make_async_remote_copy(
        src_ref=trans_hbm.at[:, pl.ds(half * (1 - c), half)], dst_ref=t_oth,
        send_sem=tsem.at[1], recv_sem=tsem.at[2], device_id=partner, device_id_type=MESH)
    oth_copy.start()

    lax.fori_loop(half * c, half * c + half, load_targets, 0)
    for h in range(HALVES):
        copy_to(0, h, 1, own_pos, half, nb_halo_pos).start()
    lax.fori_loop(half * (1 - c), half * (1 - c) + half, load_targets, 0)
    for h in range(HALVES):
        split_blocks(win0, hi0, lo0, h, half, 2 * half)

    def prep(tv, first):
        def body(k, carry):
            al = k // half
            jj = k % half
            for t in range(tv.shape[2]):
                v = jnp.transpose(tv[al, jj, t])
                b = v.astype(jnp.bfloat16)
                thi[first + al, jj, pl.ds(t * tile, tile), :] = b
                tlo[first + al, jj, pl.ds(t * tile, tile), :] = (
                    v - b.astype(jnp.float32)).astype(jnp.bfloat16)
            return carry

        lax.fori_loop(0, acts * half, body, 0)

    own_copy.wait()
    prep(t_own, 0)
    oth_copy.wait_send()
    oth_copy.wait_recv()
    prep(t_oth, acts)

    def stage(h, src, dst, first=False, halo=True):
        if first:
            done = copy_to(src, h, 1, own_pos, half, halo_pos)
            done.wait_send()
            done.wait_recv()
            split_blocks(wins[src], his[src], los[src], h, halo_pos, half)
        else:
            for k, start in ((0, part_pos), (1, halo_pos)):
                done = copy_to(src, h, k, own_pos, half, start)
                done.wait_send()
                done.wait_recv()
                split_blocks(wins[src], his[src], los[src], h, start, half)
        src_hi, src_lo = his[src], los[src]
        dst_win, dst_hi, dst_lo = wins[dst], his[dst], los[dst]

        def block(jj, carry):
            j = half * c + jj
            best = None
            for ab in range(2 * acts):
                a = lax.rem(2 * c + ab, 2 * acts)
                p0 = pos_ref[a, j, 0]
                p1 = pos_ref[a, j, 1]
                vh = jnp.concatenate([src_hi[h, p0], src_hi[h, p1]], axis=1)
                vl = jnp.concatenate([src_lo[h, p0], src_lo[h, p1]], axis=1)
                th = thi[ab, jj]
                tl = tlo[ab, jj]
                q = jnp.dot(vh, th, preferred_element_type=jnp.float32)
                q = q + jnp.dot(vl, th, preferred_element_type=jnp.float32)
                q = q + jnp.dot(vh, tl, preferred_element_type=jnp.float32)
                best = q if best is None else jnp.maximum(best, q)
            val = jnp.where(tgt_ref[h, j] == 1.0, jnp.float32(1.0), best)
            dst_win[h, own_pos + jj] = val
            if halo:
                @pl.when(jj % 2 == 1)
                def _():
                    copy_to(dst, h, 1, own_pos + jj - 1, 2, nb_halo_pos + jj - 1).start()
            copy_to(dst, h, 0, own_pos + jj, 1, own_pos + jj).start()
            b = val.astype(jnp.bfloat16)
            dst_hi[h, own_pos + jj] = b
            dst_lo[h, own_pos + jj] = (val - b.astype(jnp.float32)).astype(jnp.bfloat16)
            return carry

        lax.fori_loop(0, half, block, 0)

    for h in range(HALVES):
        stage(h, 0, 1, first=True)

    def pair(k, carry):
        for h in range(HALVES):
            stage(h, 1, 0)
        for h in range(HALVES):
            stage(h, 0, 1)
        return carry

    lax.fori_loop(0, SWEEPS // 2 - 1, pair, 0)
    for h in range(HALVES):
        stage(h, 1, 0, halo=False)

    def store_out(b, carry):
        both = jnp.concatenate([win0[h, half + b] for h in range(HALVES)], axis=0)
        out_ref[b] = jnp.transpose(both)
        return carry

    lax.fori_loop(half * c, half * c + half, store_out, 0)
    for h in range(HALVES):
        done = copy_to(0, h, 0, own_pos, half, part_pos)
        done.wait_send()
        done.wait_recv()
    lax.fori_loop(half * (1 - c), half * (1 - c) + half, store_out, 0)


def per_device(transitions, columns, targets):
    n_states = lax.axis_size("states")
    rb = transitions.shape[1]
    tile = transitions.shape[3]
    ksets = targets.shape[1]
    kh = ksets // HALVES
    total_blocks = rb * n_states
    first = lax.axis_index("states") * rb - REACH
    pos = lax.rem(columns - first + 2 * total_blocks, total_blocks).astype(jnp.int32)
    tgt = targets.reshape(rb, tile, ksets)
    half = rb // 2
    wshape = (HALVES, rb + 2 * REACH, kh, tile)
    out = pl.pallas_call(
        functools.partial(sweep_kernel, n_states),
        out_shape=jax.ShapeDtypeStruct((rb, tile, ksets), jnp.float32),
        in_specs=[
            pl.BlockSpec(memory_space=pltpu.SMEM),
            pl.BlockSpec(memory_space=pl.ANY),
            pl.BlockSpec(memory_space=pltpu.VMEM),
        ],
        out_specs=pl.BlockSpec(memory_space=pltpu.VMEM),
        scratch_shapes=[
            pltpu.VMEM(wshape, jnp.float32),
            pltpu.VMEM(wshape, jnp.float32),
            pltpu.VMEM(wshape, jnp.bfloat16),
            pltpu.VMEM(wshape, jnp.bfloat16),
            pltpu.VMEM(wshape, jnp.bfloat16),
            pltpu.VMEM(wshape, jnp.bfloat16),
            pltpu.VMEM((transitions.shape[0], half) + transitions.shape[2:], jnp.float32),
            pltpu.VMEM((transitions.shape[0], half) + transitions.shape[2:], jnp.float32),
            pltpu.VMEM((2 * transitions.shape[0], half, 2 * tile, tile), jnp.bfloat16),
            pltpu.VMEM((2 * transitions.shape[0], half, 2 * tile, tile), jnp.bfloat16),
            pltpu.VMEM((HALVES, rb, kh, tile), jnp.float32),
            pltpu.SemaphoreType.DMA((3,)),
            pltpu.SemaphoreType.DMA((2, HALVES, 2)),
            pltpu.SemaphoreType.DMA((2, HALVES, 2)),
        ],
        compiler_params=pltpu.CompilerParams(
            collective_id=0, has_side_effects=True, vmem_limit_bytes=60 * 1024 * 1024),
    )(pos, transitions, tgt)
    return out.reshape(rb * tile, ksets)


def solution(mesh):
    return jax.shard_map(
        per_device,
        mesh=mesh,
        in_specs=(P("act", "states", None, None, None), P(None, "states", None), P("states", None)),
        out_specs=P("states", None),
        check_vma=False,
    )
```

```python
import functools

import jax
import jax.numpy as jnp
from jax import lax
from jax.experimental import pallas as pl
from jax.experimental.pallas import tpu as pltpu
from jax.sharding import PartitionSpec as P

REACH = 8
SWEEPS = 12
HALVES = 2
MESH = pl.DeviceIdType.MESH


def split_blocks(src, hi, lo, h, first, count):
    def body(k, carry):
        v = src[h, first + k]
        b = v.astype(jnp.bfloat16)
        hi[h, first + k] = b
        lo[h, first + k] = (v - b.astype(jnp.float32)).astype(jnp.bfloat16)
        return carry

    lax.fori_loop(0, count, body, 0)


def sweep_kernel(n_states, pos_ref, trans_hbm, tgt_in, out_ref,
                 win0, win1, hi0, hi1, lo0, lo1, t_own, t_oth, thi, tlo, tgt_ref,
                 tsem, send_sem, recv_sem):
    i = lax.axis_index("states")
    c = lax.axis_index("act")
    acts = t_own.shape[0]
    half = t_own.shape[1]
    tile = t_own.shape[3]
    own_pos = half + half * c
    part_pos = 2 * half - half * c
    halo_pos = 3 * half * c
    nb_halo_pos = 3 * half * (1 - c)
    partner = (i, 1 - c)
    neighbour = (lax.rem(i + 2 * c - 1 + n_states, n_states), 1 - c)
    wins = (win0, win1)
    his = (hi0, hi1)
    los = (lo0, lo1)

    barrier = pltpu.get_barrier_semaphore()
    for dev in (partner, neighbour):
        pl.semaphore_signal(barrier, inc=1, device_id=dev, device_id_type=MESH)
    pl.semaphore_wait(barrier, 2)

    def copy_to(slot, h, k, start, count, dst_start):
        dev = partner if k == 0 else neighbour
        return pltpu.make_async_remote_copy(
            src_ref=wins[slot].at[h, pl.ds(start, count)],
            dst_ref=wins[slot].at[h, pl.ds(dst_start, count)],
            send_sem=send_sem.at[slot, h, k], recv_sem=recv_sem.at[slot, h, k],
            device_id=dev, device_id_type=MESH)

    kh = win0.shape[2]

    def load_targets(b, carry):
        tf = jnp.transpose(tgt_in[b].astype(jnp.float32))
        for h in range(HALVES):
            part = tf[h * kh:(h + 1) * kh]
            tgt_ref[h, b] = part
            win0[h, half + b] = part
        return carry

    own_copy = pltpu.make_async_copy(trans_hbm.at[:, pl.ds(half * c, half)], t_own, tsem.at[0])
    own_copy.start()
    oth_copies = [pltpu.make_async_remote_copy(
        src_ref=trans_hbm.at[al, pl.ds(half * (1 - c), half)], dst_ref=t_oth.at[al],
        send_sem=tsem.at[1 + 2 * al], recv_sem=tsem.at[2 + 2 * al],
        device_id=partner, device_id_type=MESH) for al in range(t_oth.shape[0])]
    for cp in oth_copies:
        cp.start()

    lax.fori_loop(half * c, half * c + half, load_targets, 0)
    for h in range(HALVES):
        copy_to(0, h, 1, own_pos, half, nb_halo_pos).start()
    lax.fori_loop(half * (1 - c), half * (1 - c) + half, load_targets, 0)
    for h in range(HALVES):
        split_blocks(win0, hi0, lo0, h, half, 2 * half)

    def prep(tv, first, a0, a1):
        def body(k, carry):
            al = a0 + k // half
            jj = k % half
            for t in range(tv.shape[2]):
                v = jnp.transpose(tv[al, jj, t])
                b = v.astype(jnp.bfloat16)
                thi[first + al, jj, pl.ds(t * tile, tile), :] = b
                tlo[first + al, jj, pl.ds(t * tile, tile), :] = (
                    v - b.astype(jnp.float32)).astype(jnp.bfloat16)
            return carry

        lax.fori_loop(0, (a1 - a0) * half, body, 0)

    own_copy.wait()
    prep(t_own, 0, 0, acts)
    for al, cp in enumerate(oth_copies):
        cp.wait_send()
        cp.wait_recv()
        prep(t_oth, acts, al, al + 1)

    def stage(h, src, dst, first=False, halo=True):
        if first:
            done = copy_to(src, h, 1, own_pos, half, halo_pos)
            done.wait_send()
            done.wait_recv()
            split_blocks(wins[src], his[src], los[src], h, halo_pos, half)
        else:
            for k, start in ((0, part_pos), (1, halo_pos)):
                done = copy_to(src, h, k, own_pos, half, start)
                done.wait_send()
                done.wait_recv()
                split_blocks(wins[src], his[src], los[src], h, start, half)
        src_hi, src_lo = his[src], los[src]
        dst_win, dst_hi, dst_lo = wins[dst], his[dst], los[dst]

        def block(jj, carry):
            j = half * c + jj
            best = None
            for ab in range(2 * acts):
                a = lax.rem(2 * c + ab, 2 * acts)
                p0 = pos_ref[a, j, 0]
                p1 = pos_ref[a, j, 1]
                vh = jnp.concatenate([src_hi[h, p0], src_hi[h, p1]], axis=1)
                vl = jnp.concatenate([src_lo[h, p0], src_lo[h, p1]], axis=1)
                th = thi[ab, jj]
                tl = tlo[ab, jj]
                q = jnp.dot(vh, th, preferred_element_type=jnp.float32)
                q = q + jnp.dot(vl, th, preferred_element_type=jnp.float32)
                q = q + jnp.dot(vh, tl, preferred_element_type=jnp.float32)
                best = q if best is None else jnp.maximum(best, q)
            val = jnp.where(tgt_ref[h, j] == 1.0, jnp.float32(1.0), best)
            dst_win[h, own_pos + jj] = val
            if halo:
                copy_to(dst, h, 1, own_pos + jj, 1, nb_halo_pos + jj).start()
            copy_to(dst, h, 0, own_pos + jj, 1, own_pos + jj).start()
            b = val.astype(jnp.bfloat16)
            dst_hi[h, own_pos + jj] = b
            dst_lo[h, own_pos + jj] = (val - b.astype(jnp.float32)).astype(jnp.bfloat16)
            return carry

        lax.fori_loop(0, half, block, 0)

    for h in range(HALVES):
        stage(h, 0, 1, first=True)

    def pair(k, carry):
        for h in range(HALVES):
            stage(h, 1, 0)
        for h in range(HALVES):
            stage(h, 0, 1)
        return carry

    lax.fori_loop(0, SWEEPS // 2 - 1, pair, 0)
    for h in range(HALVES):
        stage(h, 1, 0, halo=False)

    def store_out(b, carry):
        both = jnp.concatenate([win0[h, half + b] for h in range(HALVES)], axis=0)
        out_ref[b] = jnp.transpose(both)
        return carry

    lax.fori_loop(half * c, half * c + half, store_out, 0)
    for h in range(HALVES):
        done = copy_to(0, h, 0, own_pos, half, part_pos)
        done.wait_send()
        done.wait_recv()
    lax.fori_loop(half * (1 - c), half * (1 - c) + half, store_out, 0)


def per_device(transitions, columns, targets):
    n_states = lax.axis_size("states")
    rb = transitions.shape[1]
    tile = transitions.shape[3]
    ksets = targets.shape[1]
    kh = ksets // HALVES
    total_blocks = rb * n_states
    first = lax.axis_index("states") * rb - REACH
    pos = lax.rem(columns - first + 2 * total_blocks, total_blocks).astype(jnp.int32)
    tgt = targets.reshape(rb, tile, ksets)
    half = rb // 2
    wshape = (HALVES, rb + 2 * REACH, kh, tile)
    out = pl.pallas_call(
        functools.partial(sweep_kernel, n_states),
        out_shape=jax.ShapeDtypeStruct((rb, tile, ksets), jnp.float32),
        in_specs=[
            pl.BlockSpec(memory_space=pltpu.SMEM),
            pl.BlockSpec(memory_space=pl.ANY),
            pl.BlockSpec(memory_space=pltpu.VMEM),
        ],
        out_specs=pl.BlockSpec(memory_space=pltpu.VMEM),
        scratch_shapes=[
            pltpu.VMEM(wshape, jnp.float32),
            pltpu.VMEM(wshape, jnp.float32),
            pltpu.VMEM(wshape, jnp.bfloat16),
            pltpu.VMEM(wshape, jnp.bfloat16),
            pltpu.VMEM(wshape, jnp.bfloat16),
            pltpu.VMEM(wshape, jnp.bfloat16),
            pltpu.VMEM((transitions.shape[0], half) + transitions.shape[2:], jnp.float32),
            pltpu.VMEM((transitions.shape[0], half) + transitions.shape[2:], jnp.float32),
            pltpu.VMEM((2 * transitions.shape[0], half, 2 * tile, tile), jnp.bfloat16),
            pltpu.VMEM((2 * transitions.shape[0], half, 2 * tile, tile), jnp.bfloat16),
            pltpu.VMEM((HALVES, rb, kh, tile), jnp.float32),
            pltpu.SemaphoreType.DMA((1 + 2 * transitions.shape[0],)),
            pltpu.SemaphoreType.DMA((2, HALVES, 2)),
            pltpu.SemaphoreType.DMA((2, HALVES, 2)),
        ],
        compiler_params=pltpu.CompilerParams(
            collective_id=0, has_side_effects=True, vmem_limit_bytes=60 * 1024 * 1024),
    )(pos, transitions, tgt)
    return out.reshape(rb * tile, ksets)


def solution(mesh):
    return jax.shard_map(
        per_device,
        mesh=mesh,
        in_specs=(P("act", "states", None, None, None), P(None, "states", None), P("states", None)),
        out_specs=P("states", None),
        check_vma=False,
    )
```

```python
import functools

import jax
import jax.numpy as jnp
from jax import lax
from jax.experimental import pallas as pl
from jax.experimental.pallas import tpu as pltpu
from jax.sharding import PartitionSpec as P

REACH = 8
SWEEPS = 12
HALVES = 2
MESH = pl.DeviceIdType.MESH


def split_blocks(src, hi, lo, h, first, count):
    def body(k, carry):
        v = src[h, first + k]
        b = v.astype(jnp.bfloat16)
        hi[h, first + k] = b
        lo[h, first + k] = (v - b.astype(jnp.float32)).astype(jnp.bfloat16)
        return carry

    lax.fori_loop(0, count, body, 0)


def sweep_kernel(n_states, pos_ref, trans_hbm, tgt_in, out_ref,
                 win0, win1, hi0, hi1, lo0, lo1, t_own, t_oth, thi, tlo, tgt_ref,
                 tsem, send_sem, recv_sem):
    i = lax.axis_index("states")
    c = lax.axis_index("act")
    acts = t_own.shape[0]
    half = t_own.shape[1]
    tile = t_own.shape[3]
    own_pos = half + half * c
    part_pos = 2 * half - half * c
    halo_pos = 3 * half * c
    nb_halo_pos = 3 * half * (1 - c)
    partner = (i, 1 - c)
    neighbour = (lax.rem(i + 2 * c - 1 + n_states, n_states), 1 - c)
    wins = (win0, win1)
    his = (hi0, hi1)
    los = (lo0, lo1)

    barrier = pltpu.get_barrier_semaphore()
    for dev in (partner, neighbour):
        pl.semaphore_signal(barrier, inc=1, device_id=dev, device_id_type=MESH)
    pl.semaphore_wait(barrier, 2)

    def copy_to(slot, h, k, start, count, dst_start):
        dev = partner if k == 0 else neighbour
        return pltpu.make_async_remote_copy(
            src_ref=wins[slot].at[h, pl.ds(start, count)],
            dst_ref=wins[slot].at[h, pl.ds(dst_start, count)],
            send_sem=send_sem.at[slot, h, k], recv_sem=recv_sem.at[slot, h, k],
            device_id=dev, device_id_type=MESH)

    kh = win0.shape[2]

    def load_targets(b, carry):
        tf = jnp.transpose(tgt_in[b].astype(jnp.float32))
        for h in range(HALVES):
            part = tf[h * kh:(h + 1) * kh]
            tgt_ref[h, b] = part
            win0[h, half + b] = part
        return carry

    own_copy = pltpu.make_async_copy(trans_hbm.at[:, pl.ds(half * c, half)], t_own, tsem.at[0])
    own_copy.start()
    oth_copy = pltpu.make_async_remote_copy(
        src_ref=trans_hbm.at[:, pl.ds(half * (1 - c), half)], dst_ref=t_oth,
        send_sem=tsem.at[1], recv_sem=tsem.at[2], device_id=partner, device_id_type=MESH)
    oth_copy.start()

    lax.fori_loop(half * c, half * c + half, load_targets, 0)
    for h in range(HALVES):
        copy_to(0, h, 1, own_pos, half, nb_halo_pos).start()
    lax.fori_loop(half * (1 - c), half * (1 - c) + half, load_targets, 0)
    for h in range(HALVES):
        split_blocks(win0, hi0, lo0, h, half, 2 * half)

    def prep(tv, first):
        def body(k, carry):
            al = k // half
            jj = k % half
            for t in range(tv.shape[2]):
                v = jnp.transpose(tv[al, jj, t])
                b = v.astype(jnp.bfloat16)
                thi[first + al, jj, pl.ds(t * tile, tile), :] = b
                tlo[first + al, jj, pl.ds(t * tile, tile), :] = (
                    v - b.astype(jnp.float32)).astype(jnp.bfloat16)
            return carry

        lax.fori_loop(0, acts * half, body, 0)

    own_copy.wait()
    prep(t_own, 0)
    oth_copy.wait_send()
    oth_copy.wait_recv()
    prep(t_oth, acts)

    def stage(h, src, dst, first=False, halo=True):
        links = ((1, halo_pos),) if first else ((0, part_pos), (1, halo_pos))
        for k, start in links:
            copy_to(src, h, k, own_pos, half, start).wait_recv()
            split_blocks(wins[src], his[src], los[src], h, start, half)
        src_hi, src_lo = his[src], los[src]
        dst_win, dst_hi, dst_lo = wins[dst], his[dst], los[dst]

        def block(jj, carry):
            j = half * c + jj
            best = None
            for ab in range(2 * acts):
                a = lax.rem(2 * c + ab, 2 * acts)
                p0 = pos_ref[a, j, 0]
                p1 = pos_ref[a, j, 1]
                vh = jnp.concatenate([src_hi[h, p0], src_hi[h, p1]], axis=1)
                vl = jnp.concatenate([src_lo[h, p0], src_lo[h, p1]], axis=1)
                th = thi[ab, jj]
                tl = tlo[ab, jj]
                q = jnp.dot(vh, th, preferred_element_type=jnp.float32)
                q = q + jnp.dot(vl, th, preferred_element_type=jnp.float32)
                q = q + jnp.dot(vh, tl, preferred_element_type=jnp.float32)
                best = q if best is None else jnp.maximum(best, q)
            val = jnp.where(tgt_ref[h, j] == 1.0, jnp.float32(1.0), best)
            dst_win[h, own_pos + jj] = val
            if halo:
                copy_to(dst, h, 1, own_pos + jj, 1, nb_halo_pos + jj).start()
            copy_to(dst, h, 0, own_pos + jj, 1, own_pos + jj).start()
            b = val.astype(jnp.bfloat16)
            dst_hi[h, own_pos + jj] = b
            dst_lo[h, own_pos + jj] = (val - b.astype(jnp.float32)).astype(jnp.bfloat16)
            return carry

        lax.fori_loop(0, half, block, 0)
        for k, start in links:
            copy_to(src, h, k, own_pos, half, start).wait_send()

    for h in range(HALVES):
        stage(h, 0, 1, first=True)

    def pair(k, carry):
        for h in range(HALVES):
            stage(h, 1, 0)
        for h in range(HALVES):
            stage(h, 0, 1)
        return carry

    lax.fori_loop(0, SWEEPS // 2 - 1, pair, 0)
    for h in range(HALVES):
        stage(h, 1, 0, halo=False)

    def store_out(b, carry):
        both = jnp.concatenate([win0[h, half + b] for h in range(HALVES)], axis=0)
        out_ref[b] = jnp.transpose(both)
        return carry

    lax.fori_loop(half * c, half * c + half, store_out, 0)
    for h in range(HALVES):
        done = copy_to(0, h, 0, own_pos, half, part_pos)
        done.wait_send()
        done.wait_recv()
    lax.fori_loop(half * (1 - c), half * (1 - c) + half, store_out, 0)


def per_device(transitions, columns, targets):
    n_states = lax.axis_size("states")
    rb = transitions.shape[1]
    tile = transitions.shape[3]
    ksets = targets.shape[1]
    kh = ksets // HALVES
    total_blocks = rb * n_states
    first = lax.axis_index("states") * rb - REACH
    pos = lax.rem(columns - first + 2 * total_blocks, total_blocks).astype(jnp.int32)
    tgt = targets.reshape(rb, tile, ksets)
    half = rb // 2
    wshape = (HALVES, rb + 2 * REACH, kh, tile)
    out = pl.pallas_call(
        functools.partial(sweep_kernel, n_states),
        out_shape=jax.ShapeDtypeStruct((rb, tile, ksets), jnp.float32),
        in_specs=[
            pl.BlockSpec(memory_space=pltpu.SMEM),
            pl.BlockSpec(memory_space=pl.ANY),
            pl.BlockSpec(memory_space=pltpu.VMEM),
        ],
        out_specs=pl.BlockSpec(memory_space=pltpu.VMEM),
        scratch_shapes=[
            pltpu.VMEM(wshape, jnp.float32),
            pltpu.VMEM(wshape, jnp.float32),
            pltpu.VMEM(wshape, jnp.bfloat16),
            pltpu.VMEM(wshape, jnp.bfloat16),
            pltpu.VMEM(wshape, jnp.bfloat16),
            pltpu.VMEM(wshape, jnp.bfloat16),
            pltpu.VMEM((transitions.shape[0], half) + transitions.shape[2:], jnp.float32),
            pltpu.VMEM((transitions.shape[0], half) + transitions.shape[2:], jnp.float32),
            pltpu.VMEM((2 * transitions.shape[0], half, 2 * tile, tile), jnp.bfloat16),
            pltpu.VMEM((2 * transitions.shape[0], half, 2 * tile, tile), jnp.bfloat16),
            pltpu.VMEM((HALVES, rb, kh, tile), jnp.float32),
            pltpu.SemaphoreType.DMA((3,)),
            pltpu.SemaphoreType.DMA((2, HALVES, 2)),
            pltpu.SemaphoreType.DMA((2, HALVES, 2)),
        ],
        compiler_params=pltpu.CompilerParams(
            collective_id=0, has_side_effects=True, vmem_limit_bytes=60 * 1024 * 1024),
    )(pos, transitions, tgt)
    return out.reshape(rb * tile, ksets)


def solution(mesh):
    return jax.shard_map(
        per_device,
        mesh=mesh,
        in_specs=(P("act", "states", None, None, None), P(None, "states", None), P("states", None)),
        out_specs=P("states", None),
        check_vma=False,
    )
```

```python
import functools

import jax
import jax.numpy as jnp
from jax import lax
from jax.experimental import pallas as pl
from jax.experimental.pallas import tpu as pltpu
from jax.sharding import PartitionSpec as P

REACH = 8
SWEEPS = 12
HALVES = 2
MESH = pl.DeviceIdType.MESH


def split_blocks(src, hi, lo, h, first, count):
    def body(k, carry):
        v = src[h, first + k]
        b = v.astype(jnp.bfloat16)
        hi[h, first + k] = b
        lo[h, first + k] = (v - b.astype(jnp.float32)).astype(jnp.bfloat16)
        return carry

    lax.fori_loop(0, count, body, 0)


def sweep_kernel(n_states, pos_ref, trans_hbm, tgt_in, out_ref,
                 win0, win1, hi0, hi1, lo0, lo1, t_own, t_oth, thi, tlo, tgt_ref,
                 tsem, send_sem, recv_sem):
    i = lax.axis_index("states")
    c = lax.axis_index("act")
    acts = t_own.shape[0]
    half = t_own.shape[1]
    tile = t_own.shape[3]
    own_pos = half + half * c
    part_pos = 2 * half - half * c
    halo_pos = 3 * half * c
    nb_halo_pos = 3 * half * (1 - c)
    partner = (i, 1 - c)
    neighbour = (lax.rem(i + 2 * c - 1 + n_states, n_states), 1 - c)
    wins = (win0, win1)
    his = (hi0, hi1)
    los = (lo0, lo1)

    barrier = pltpu.get_barrier_semaphore()
    for dev in (partner, neighbour):
        pl.semaphore_signal(barrier, inc=1, device_id=dev, device_id_type=MESH)
    pl.semaphore_wait(barrier, 2)

    def copy_to(slot, h, k, start, count, dst_start):
        dev = partner if k == 0 else neighbour
        return pltpu.make_async_remote_copy(
            src_ref=wins[slot].at[h, pl.ds(start, count)],
            dst_ref=wins[slot].at[h, pl.ds(dst_start, count)],
            send_sem=send_sem.at[slot, h, k], recv_sem=recv_sem.at[slot, h, k],
            device_id=dev, device_id_type=MESH)

    kh = win0.shape[2]

    def load_targets(b, carry):
        tf = jnp.transpose(tgt_in[b].astype(jnp.float32))
        for h in range(HALVES):
            part = tf[h * kh:(h + 1) * kh]
            tgt_ref[h, b] = part
            win0[h, half + b] = part
        return carry

    own_copy = pltpu.make_async_copy(trans_hbm.at[:, pl.ds(half * c, half)], t_own, tsem.at[0])
    own_copy.start()
    oth_copy = pltpu.make_async_remote_copy(
        src_ref=trans_hbm.at[:, pl.ds(half * (1 - c), half)], dst_ref=t_oth,
        send_sem=tsem.at[1], recv_sem=tsem.at[2], device_id=partner, device_id_type=MESH)
    oth_copy.start()

    lax.fori_loop(half * c, half * c + half, load_targets, 0)
    for h in range(HALVES):
        copy_to(0, h, 1, own_pos, half, nb_halo_pos).start()
    lax.fori_loop(half * (1 - c), half * (1 - c) + half, load_targets, 0)
    for h in range(HALVES):
        split_blocks(win0, hi0, lo0, h, half, 2 * half)

    def prep(tv, first):
        def body(k, carry):
            al = k // half
            jj = k % half
            for t in range(tv.shape[2]):
                v = jnp.transpose(tv[al, jj, t])
                b = v.astype(jnp.bfloat16)
                thi[first + al, jj, pl.ds(t * tile, tile), :] = b
                tlo[first + al, jj, pl.ds(t * tile, tile), :] = (
                    v - b.astype(jnp.float32)).astype(jnp.bfloat16)
            return carry

        lax.fori_loop(0, acts * half, body, 0)

    own_copy.wait()
    prep(t_own, 0)
    oth_copy.wait_send()
    oth_copy.wait_recv()
    prep(t_oth, acts)

    def stage(h, src, dst, first=False, halo=True):
        links = ((1, halo_pos),) if first else ((1, halo_pos), (0, part_pos))
        for k, start in links:
            copy_to(src, h, k, own_pos, half, start).wait_recv()
            split_blocks(wins[src], his[src], los[src], h, start, half)
        src_hi, src_lo = his[src], los[src]
        dst_win, dst_hi, dst_lo = wins[dst], his[dst], los[dst]

        def block(jj, carry):
            j = half * c + jj
            best = None
            for ab in range(2 * acts):
                a = lax.rem(2 * c + ab, 2 * acts)
                p0 = pos_ref[a, j, 0]
                p1 = pos_ref[a, j, 1]
                vh = jnp.concatenate([src_hi[h, p0], src_hi[h, p1]], axis=1)
                vl = jnp.concatenate([src_lo[h, p0], src_lo[h, p1]], axis=1)
                th = thi[ab, jj]
                tl = tlo[ab, jj]
                q = jnp.dot(vh, th, preferred_element_type=jnp.float32)
                q = q + jnp.dot(vl, th, preferred_element_type=jnp.float32)
                q = q + jnp.dot(vh, tl, preferred_element_type=jnp.float32)
                best = q if best is None else jnp.maximum(best, q)
            val = jnp.where(tgt_ref[h, j] == 1.0, jnp.float32(1.0), best)
            dst_win[h, own_pos + jj] = val
            if halo:
                copy_to(dst, h, 1, own_pos + jj, 1, nb_halo_pos + jj).start()
            copy_to(dst, h, 0, own_pos + jj, 1, own_pos + jj).start()
            b = val.astype(jnp.bfloat16)
            dst_hi[h, own_pos + jj] = b
            dst_lo[h, own_pos + jj] = (val - b.astype(jnp.float32)).astype(jnp.bfloat16)
            return carry

        lax.fori_loop(0, half, block, 0)
        for k, start in links:
            copy_to(src, h, k, own_pos, half, start).wait_send()

    for h in range(HALVES):
        stage(h, 0, 1, first=True)

    def pair(k, carry):
        for h in range(HALVES):
            stage(h, 1, 0)
        for h in range(HALVES):
            stage(h, 0, 1)
        return carry

    lax.fori_loop(0, SWEEPS // 2 - 1, pair, 0)
    for h in range(HALVES):
        stage(h, 1, 0, halo=False)

    def store_out(b, carry):
        both = jnp.concatenate([win0[h, half + b] for h in range(HALVES)], axis=0)
        out_ref[b] = jnp.transpose(both)
        return carry

    lax.fori_loop(half * c, half * c + half, store_out, 0)
    for h in range(HALVES):
        done = copy_to(0, h, 0, own_pos, half, part_pos)
        done.wait_send()
        done.wait_recv()
    lax.fori_loop(half * (1 - c), half * (1 - c) + half, store_out, 0)


def per_device(transitions, columns, targets):
    n_states = lax.axis_size("states")
    rb = transitions.shape[1]
    tile = transitions.shape[3]
    ksets = targets.shape[1]
    kh = ksets // HALVES
    total_blocks = rb * n_states
    first = lax.axis_index("states") * rb - REACH
    pos = lax.rem(columns - first + 2 * total_blocks, total_blocks).astype(jnp.int32)
    tgt = targets.reshape(rb, tile, ksets)
    half = rb // 2
    wshape = (HALVES, rb + 2 * REACH, kh, tile)
    out = pl.pallas_call(
        functools.partial(sweep_kernel, n_states),
        out_shape=jax.ShapeDtypeStruct((rb, tile, ksets), jnp.float32),
        in_specs=[
            pl.BlockSpec(memory_space=pltpu.SMEM),
            pl.BlockSpec(memory_space=pl.ANY),
            pl.BlockSpec(memory_space=pltpu.VMEM),
        ],
        out_specs=pl.BlockSpec(memory_space=pltpu.VMEM),
        scratch_shapes=[
            pltpu.VMEM(wshape, jnp.float32),
            pltpu.VMEM(wshape, jnp.float32),
            pltpu.VMEM(wshape, jnp.bfloat16),
            pltpu.VMEM(wshape, jnp.bfloat16),
            pltpu.VMEM(wshape, jnp.bfloat16),
            pltpu.VMEM(wshape, jnp.bfloat16),
            pltpu.VMEM((transitions.shape[0], half) + transitions.shape[2:], jnp.float32),
            pltpu.VMEM((transitions.shape[0], half) + transitions.shape[2:], jnp.float32),
            pltpu.VMEM((2 * transitions.shape[0], half, 2 * tile, tile), jnp.bfloat16),
            pltpu.VMEM((2 * transitions.shape[0], half, 2 * tile, tile), jnp.bfloat16),
            pltpu.VMEM((HALVES, rb, kh, tile), jnp.float32),
            pltpu.SemaphoreType.DMA((3,)),
            pltpu.SemaphoreType.DMA((2, HALVES, 2)),
            pltpu.SemaphoreType.DMA((2, HALVES, 2)),
        ],
        compiler_params=pltpu.CompilerParams(
            collective_id=0, has_side_effects=True, vmem_limit_bytes=60 * 1024 * 1024),
    )(pos, transitions, tgt)
    return out.reshape(rb * tile, ksets)


def solution(mesh):
    return jax.shard_map(
        per_device,
        mesh=mesh,
        in_specs=(P("act", "states", None, None, None), P(None, "states", None), P("states", None)),
        out_specs=P("states", None),
        check_vma=False,
    )
```
